128 devices in a mesh: sec: 16 (over y, x), dev: 8 (over z, core).
Axes of the slice: x: 4, y: 4, z: 4, core: 2. Of those that a mesh axis runs over, the one named last changes fastest.
Arguments:
- rhs_interior: bfloat16 [1310720, 256], P(('sec', 'dev')), may hold values from -6 to 6
- rhs_interface: float32 [10240, 256], P(('sec', 'dev')), may hold values from -6 to 6
- inv_blocks: bfloat16 [5120, 256, 256], P(('sec', 'dev')), may hold values from -0.375 to 0.375
- coupling: bfloat16 [5120, 2, 64, 256], P(('sec', 'dev')), may hold values from -0.1875 to 0.1875
- interface_map: int32 [5120, 64], P(('sec', 'dev')), may hold values from 0 to 10239, as said below
- slot_counts: int32 [5120], P(('sec', 'dev')), may hold values from 32 to 64, as said below
- column_order: int32 [256], replicated, may hold values from 0 to 255, each once
- schur_inverse: bfloat16 [10240, 10240], P('dev', 'sec'), may hold values from -0.0625 to 0.0625
Outputs:
- interior_solution: bfloat16 [1310720, 256], P(('sec', 'dev'))
- interface_solution: float32 [10240, 256], P('dev')
The draws below stay inside these ranges and needn't reach their ends.
Inputs may be any that keep to these rules, and one draw needn't show every extreme that they name: `slot_counts`: every block has at least half of its 64 slots live, and some block has all 64 live. `interface_map`: split the interface rows into 128 equal ranges, range d belonging to the device of flat index d over sec+dev; of the 2560 slots of one device's blocks at most 40 point into any one range, the slots into ranges 2p and 2p + 1 together number exactly 40, and one range receives exactly 40 slots from every device.
All inputs are finite; a program needn't handle non-finite values.
Results may differ from the reference program's by a relative error of at most 0.0056.
Values may be sent and summed in bfloat16 or wider, within the bound.
No kernel may reach another device: no remote copies, remote signals or barrier semaphores. Data moves between devices by JAX's collectives and lax.ppermute only.
A program may use at most 128 MiB of HBM per device.

```python
import jax
import jax.numpy as jnp
from jax import lax

B = 256
K = 64
NI = 10240
NBD = 40
NCOL = 256
NBLK = 5120
NU = 1310720


def draw_slot_counts(key, part):
    count_key = jax.random.fold_in(key, 11)
    spot_key = jax.random.fold_in(key, 12)
    counts = jax.random.randint(count_key, (NBLK,), K // 2, K + 1)
    spot = jax.random.randint(spot_key, (), 0, NBLK)
    return counts.at[spot].set(K).astype(jnp.int32)


def draw_interface_map(key, part):
    owners = NBLK // NBD
    per_owner = NBD * K
    capacity = 2 * per_owner // owners
    piece = NI // owners
    pairs = owners // 2
    spot = jax.random.randint(jax.random.fold_in(key, 21), (), 0, pairs)
    lower = jax.random.randint(jax.random.fold_in(key, 22), (owners, pairs), capacity // 4, capacity - capacity // 4 + 1)
    lower = lower.at[:, spot].set(0)
    position = jnp.arange(capacity, dtype=jnp.int32)
    pair_index = jnp.arange(pairs, dtype=jnp.int32)
    target_owner = 2 * pair_index[None, :, None] + (position[None, None, :] >= lower[:, :, None]).astype(jnp.int32)
    target_owner = target_owner.reshape(owners, per_owner)
    shuffle_keys = jax.random.split(jax.random.fold_in(key, 23), owners)
    target_owner = jax.vmap(lambda one_key, row: jax.random.permutation(one_key, row))(shuffle_keys, target_owner)
    offsets = jax.random.randint(jax.random.fold_in(key, 24), (owners, per_owner), 0, piece)
    rows = target_owner * piece + offsets
    return rows.reshape(NBLK, K).astype(jnp.int32)


def block_scale(own_key, extent, pieces, least, high):
    gain, own = 1.0, jax.random.fold_in(own_key, 6)
    for dim, parts in pieces:
        draws = jnp.exp(jax.random.uniform(jax.random.fold_in(own, dim), (parts,), jnp.float32, least / len(pieces), high / len(pieces)))
        gain = gain * jnp.repeat(draws, extent[dim] // parts).reshape([-1 if axis == dim else 1 for axis in range(len(extent))])
    return gain


def centred(own_key, dims, width, most, cuts=(), kind=jnp.bfloat16):
    result = width * jax.random.normal(own_key, dims, jnp.float32)
    if cuts:
        result = result * block_scale(own_key, dims, cuts, -0.22, 0.18)
    return jnp.clip(result, -most, most).astype(kind)


def setup_inputs(seed: int = 0) -> dict:
    key_of = jax.random.split(jax.random.key(seed), 9)
    rhs_interior = centred(key_of[0], (NU, NCOL), 1.0, 6.0, ((0, 128),))
    rhs_interface = centred(key_of[1], (NI, NCOL), 1.0, 6.0, ((0, 128),), jnp.float32)
    inv_blocks = centred(key_of[2], (NBLK, B, B), B ** -0.5, 0.375, ((0, 128),))
    coupling = centred(key_of[3], (NBLK, 2, K, B), (4 * B) ** -0.5, 0.1875, ((0, 128),))
    interface_map = draw_interface_map(jax.random.fold_in(key_of[8], 71), 0)
    slot_counts = draw_slot_counts(jax.random.fold_in(key_of[8], 71), 0)
    column_order = jax.random.permutation(key_of[6], NCOL).astype(jnp.int32)
    schur_inverse = centred(key_of[7], (NI, NI), NI ** -0.5, 0.0625, ((0, 8), (1, 16)))
    return dict(rhs_interior=rhs_interior, rhs_interface=rhs_interface, inv_blocks=inv_blocks, coupling=coupling, interface_map=interface_map, slot_counts=slot_counts, column_order=column_order, schur_inverse=schur_inverse)


def reference(rhs_interior, rhs_interface, inv_blocks, coupling, interface_map, slot_counts, column_order, schur_inverse):
    live_mask = (jnp.arange(K, dtype=jnp.int32)[None, :] < slot_counts[:, None]).astype(jnp.float32)
    rhs_cols = jnp.take(rhs_interface, column_order, axis=1)
    groups = NBLK // NBD
    rhs_groups = rhs_interior.reshape(groups, NBD, B, NCOL)
    inv_groups = inv_blocks.reshape(groups, NBD, B, B)
    coupling_groups = coupling.reshape(groups, NBD, 2, K, B)
    map_groups = interface_map.reshape(groups, NBD * K)
    mask_groups = live_mask.reshape(groups, NBD, K)

    def forward(running, inputs):
        rhs_part, inv_part, coupling_part, map_part, mask_part = inputs
        solved = jnp.einsum("bij,bjn->bin", inv_part.astype(jnp.float32), rhs_part.astype(jnp.float32)).astype(jnp.bfloat16)
        solved = lax.optimization_barrier(solved)
        partials = jnp.einsum("bkr,brn->bkn", coupling_part[:, 0].astype(jnp.float32), solved.astype(jnp.float32))
        partials = partials * mask_part[:, :, None]
        running = running.at[map_part].add(-partials.reshape(NBD * K, NCOL))
        return running, solved

    scattered, solved_all = lax.scan(forward, jnp.zeros((NI, NCOL), jnp.float32), (rhs_groups, inv_groups, coupling_groups, map_groups, mask_groups))
    reduced = rhs_cols + scattered
    reduced_bf = reduced.astype(jnp.bfloat16)
    interface_solution = jnp.dot(schur_inverse, reduced_bf, preferred_element_type=jnp.float32)
    values = lax.optimization_barrier(interface_solution.astype(jnp.bfloat16))

    def backward(inputs):
        solved, inv_part, coupling_part, map_part, mask_part = inputs
        picked = jnp.take(values, map_part, axis=0).reshape(NBD, K, NCOL) * mask_part[:, :, None].astype(jnp.bfloat16)
        pushed = jnp.einsum("bkr,bkn->brn", coupling_part[:, 1].astype(jnp.float32), picked.astype(jnp.float32)).astype(jnp.bfloat16)
        pushed = lax.optimization_barrier(pushed)
        back_term = jnp.einsum("bij,bjn->bin", inv_part.astype(jnp.float32), pushed.astype(jnp.float32))
        return (solved.astype(jnp.float32) - back_term).astype(jnp.bfloat16)

    interior = lax.map(backward, (solved_all, inv_groups, coupling_groups, map_groups, mask_groups))
    return interior.reshape(NU, NCOL), interface_solution
```

```python
import jax
import jax.numpy as jnp
from jax import lax
from jax.sharding import Mesh
from jax.sharding import PartitionSpec as P

ALL = ("y", "x", "z", "c")
SEC = ("y", "x")
DEV = ("z", "c")
WIRE = 24


def exchange(blocks, axis):
    return lax.all_to_all(blocks, axis, 0, 0, tiled=True)


def copies(array, axis):
    size = lax.axis_size(axis)
    return exchange(jnp.broadcast_to(array[None], (size, *array.shape)), axis)


def strict_lower(n):
    return (jnp.arange(n)[:, None] > jnp.arange(n)[None, :]).astype(jnp.bfloat16)


def shards(
    rhs_interior,
    rhs_interface,
    inv_blocks,
    coupling,
    interface_map,
    slot_counts,
    column_order,
    schur_inverse,
):
    f32, bf16 = jnp.float32, jnp.bfloat16
    nb, n = inv_blocks.shape[:2]
    k = coupling.shape[2]
    cols = rhs_interior.shape[1]
    owners = lax.axis_size(ALL)
    devs = lax.axis_size(DEV)
    secs = lax.axis_size(SEC)
    pairs = owners // 2
    slots = nb * k
    per_pair = slots // pairs
    half = per_pair // 2
    piece = rhs_interface.shape[0]
    pair_rows = 2 * piece
    band = piece * secs
    live = jnp.arange(k, dtype=jnp.int32)[None, :] < slot_counts[:, None]

    pair = interface_map // pair_rows
    off = interface_map % pair_rows
    table = (pair[:, :, None] == jnp.arange(pairs, dtype=jnp.int32)).astype(bf16)
    within = jnp.einsum("kj,bjp->bkp", strict_lower(k), table, preferred_element_type=f32)
    counts = jnp.sum(table.astype(f32), axis=1)
    base = jnp.dot(strict_lower(nb), counts.astype(bf16), preferred_element_type=f32)
    rank = jnp.sum((within + base[:, None, :]) * table.astype(f32), axis=-1).astype(jnp.int32)
    place = (pair * per_pair + rank).reshape(-1)
    wire_place = (place // half) * WIRE + place % half

    solved = jnp.einsum(
        "bij,bjn->bin",
        inv_blocks,
        rhs_interior.reshape(nb, n, cols),
        preferred_element_type=f32,
    ).astype(bf16)
    partials = jnp.einsum("bkr,brn->bkn", coupling[:, 0], solved, preferred_element_type=f32)
    partials = jnp.where(live[:, :, None], partials, 0.0).astype(bf16).reshape(slots, cols)

    mover = jnp.arange(owners * WIRE, dtype=jnp.int32)[:, None] == wire_place[None, :]
    rows = jnp.dot(mover.astype(bf16), partials, preferred_element_type=f32).astype(bf16)
    offs = jnp.sum(jnp.where(mover, off.reshape(1, -1), 0), axis=1).astype(bf16)
    offs = offs.reshape(owners, WIRE)
    spare = jnp.arange(WIRE) >= half
    row_index = jnp.where(spare, -1.0, offs).astype(bf16)
    row_index = jnp.pad(row_index, ((0, 0), (0, cols - WIRE)))[:, None, :]
    wanted = offs[:, :half].reshape(devs, 2, band // pair_rows // 2 * per_pair)
    wanted = jnp.pad(wanted, ((0, 0), (0, 0), (0, cols - wanted.shape[2])))
    wanted = jnp.broadcast_to(wanted[None], (secs, *wanted.shape)).reshape(owners, 2, cols)
    rows = rows.reshape(owners, WIRE, cols)
    sent = jnp.concatenate([rows[:, :half], row_index, wanted, rows[:, half + 3 :]], axis=1)
    got = exchange(sent, ALL)

    target = got[:, half, :WIRE].reshape(1, -1)
    selector = jnp.arange(pair_rows, dtype=jnp.int32)[:, None].astype(bf16) == target
    arrived = jnp.dot(
        selector.astype(bf16), got.reshape(-1, cols), preferred_element_type=f32
    ).reshape(2, piece, cols)
    rhs_cols = jnp.take(rhs_interface, column_order, axis=1)
    mine = jnp.arange(2)[:, None, None] == lax.axis_index("c")
    own = jnp.where(mine, rhs_cols[None], 0.0) - arrived
    reduced = own + lax.ppermute(own, "c", [(0, 1), (1, 0)])
    reduced = reduced.reshape(pair_rows, cols).astype(bf16)
    section = copies(reduced, "z").reshape(-1, cols)

    product = jnp.dot(schur_inverse, section, preferred_element_type=f32)
    parts = exchange(product.astype(bf16).reshape(secs, piece, cols), SEC)
    summed = jnp.sum(parts.astype(f32), axis=0).astype(bf16)
    values = copies(summed, SEC).reshape(band, cols)

    s = lax.axis_index(SEC)
    asked = lax.dynamic_slice_in_dim(got, s * devs, devs, axis=0)[
        :, half + 1 : half + 3, : per_pair * (band // pair_rows) // 2
    ].reshape(devs, band // pair_rows, per_pair)
    picker = asked[:, :, :, None] == jnp.arange(pair_rows, dtype=jnp.int32).astype(bf16)
    returned = jnp.einsum(
        "vjkr,jrn->vjkn",
        picker.astype(bf16),
        values.reshape(-1, pair_rows, cols),
        preferred_element_type=f32,
    ).astype(bf16)
    back = exchange(returned.reshape(devs, -1, cols), DEV).reshape(slots, cols)

    unmover = place[:, None] == jnp.arange(slots, dtype=jnp.int32)[None, :]
    picked = jnp.dot(unmover.astype(bf16), back, preferred_element_type=f32).astype(bf16)
    picked = jnp.where(live[:, :, None], picked.reshape(nb, k, cols), jnp.zeros((), bf16))
    pushed = jnp.einsum(
        "bkr,bkn->brn", coupling[:, 1], picked, preferred_element_type=f32
    ).astype(bf16)
    back_term = jnp.einsum("bij,bjn->bin", inv_blocks, pushed, preferred_element_type=f32)
    interior = (solved.astype(f32) - back_term).astype(bf16)
    return interior.reshape(nb * n, cols), values.astype(f32)


def solution(mesh):
    fine = Mesh(mesh.devices.reshape(4, 4, 4, 2), ALL)
    placed = (
        P(ALL, None),
        P(ALL, None),
        P(ALL, None, None),
        P(ALL, None, None, None),
        P(ALL, None),
        P(ALL),
        P(),
        P(DEV, SEC),
    )
    return jax.shard_map(
        shards,
        mesh=fine,
        in_specs=placed,
        out_specs=(P(ALL, None), P(DEV, None)),
        check_vma=False,
    )
```

```python
import functools

import jax
import jax.numpy as jnp
from jax import lax
from jax.experimental import pallas as pl
from jax.experimental.pallas import tpu as pltpu
from jax.sharding import Mesh
from jax.sharding import PartitionSpec as P

ALL = ("y", "x", "z", "c")
SEC = ("y", "x")
DEV = ("z", "c")
WIRE = 24
DEAD = 16384
GROUP = 4
F32, BF16 = jnp.float32, jnp.bfloat16


def exchange(blocks, axis):
    return lax.all_to_all(blocks, axis, 0, 0, tiled=True)


def copies(array, axis):
    size = lax.axis_size(axis)
    return exchange(jnp.broadcast_to(array[None], (size, *array.shape)), axis)


def iota(shape, dim):
    return lax.broadcasted_iota(jnp.int32, shape, dim).astype(F32)


def quotient(x, n):
    return jnp.floor((x + 0.5) * (1.0 / n))


def dot(a, b, dims=((1,), (0,))):
    return lax.dot_general(a, b, (dims, ((), ())), preferred_element_type=F32)


def onehot(mask):
    return jnp.where(mask, 1.0, 0.0).astype(BF16)


def forward_kernel(
    sizes, map_ref, rhs_ref, inv_ref, couple_ref, out_ref, place_ref, base_ref, offs_ref
):
    per_pair, half, pair_rows, pairs, devs = sizes
    step = pl.program_id(0)
    n = inv_ref.shape[1]
    k = couple_ref.shape[1]
    lanes = GROUP * k
    tile = 256
    tiles = out_ref.shape[0] // tile

    @pl.when(step == 0)
    def _():
        base_ref[...] = jnp.zeros_like(base_ref)
        offs_ref[...] = jnp.zeros_like(offs_ref)
        out_ref[...] = jnp.zeros_like(out_ref)

    slot = map_ref[0].astype(F32)
    dead = slot >= DEAD
    slot = jnp.where(dead, slot - DEAD, slot)
    pair = quotient(slot, pair_rows)
    off = slot - pair_rows * pair
    table = jnp.where(iota((pairs, lanes), 0) == pair, 1.0, 0.0)
    before = dot(
        table.astype(BF16), onehot(iota((lanes, lanes), 0) < iota((lanes, lanes), 1))
    )
    rank = jnp.sum(table * (before + base_ref[:, :1]), axis=0, keepdims=True)
    base_ref[...] += jnp.sum(table, axis=1, keepdims=True)
    place = pair * per_pair + rank
    place_ref[0] = jnp.where(dead, -1.0, place)
    wire = jnp.where(dead, -1.0, place + (WIRE - half) * quotient(place, half))
    row64 = lax.broadcasted_iota(jnp.int32, (256, lanes), 0) & 63
    offs_ref[...] += dot(
        (table * off).astype(BF16), onehot(row64.astype(F32) == rank), ((1,), (1,))
    )

    parts = []
    for b in range(GROUP):
        solved = dot(inv_ref[b], rhs_ref[b * n : (b + 1) * n, :]).astype(BF16)
        parts.append(dot(couple_ref[b], solved).astype(BF16))
    partials = jnp.concatenate(parts, axis=0)
    for t in range(tiles):
        mover = onehot(iota((tile, lanes), 0) == wire - float(tile * t))
        rows = slice(tile * t, tile * (t + 1))
        out_ref[rows, :] = out_ref[rows, :] + dot(mover, partials).astype(BF16)

    @pl.when(step == pl.num_programs(0) - 1)
    def _():
        offs = offs_ref[...]
        p = lax.broadcasted_iota(jnp.int32, offs.shape, 0)
        lane = lax.broadcasted_iota(jnp.int32, offs.shape, 1)
        spread = jnp.where((lane >> 6) == (p & 3), offs, 0.0).astype(BF16)
        groups = pairs // 4
        wanted = dot(
            onehot(iota((groups, pairs), 0) == quotient(iota((groups, pairs), 1), 4)), spread
        )
        rest = 128 - pairs - groups
        index = jnp.concatenate(
            [offs, wanted, jnp.zeros((rest, offs.shape[1]), F32)], axis=0
        ).astype(BF16)
        for t in range(tiles):
            w = iota((tile, 128), 0) + float(tile * t)
            d = quotient(w, WIRE)
            r = w - WIRE * d
            v = d - devs * quotient(d, devs)
            chosen = jnp.where(
                r == half,
                quotient(d, 2),
                jnp.where(
                    r == half + 1,
                    pairs + 2 * v,
                    jnp.where(r == half + 2, pairs + 1 + 2 * v, -1.0),
                ),
            )
            rows = slice(tile * t, tile * (t + 1))
            picker = onehot(iota((tile, 128), 1) == chosen)
            out_ref[rows, :] = out_ref[rows, :] + dot(picker, index).astype(BF16)


def middle_kernel(rhs_ref, inv_ref, couple_ref, solved_ref, w_ref):
    n = inv_ref.shape[1]
    for b in range(inv_ref.shape[0]):
        rows = slice(b * n, (b + 1) * n)
        solved_ref[rows, :] = dot(inv_ref[b], rhs_ref[rows, :]).astype(BF16)
        w_ref[b] = dot(inv_ref[b], couple_ref[b], ((1,), (1,))).astype(BF16)


def tail_kernel(place_ref, back_ref, solved_ref, w_ref, out_ref):
    n = w_ref.shape[1]
    k = w_ref.shape[2]
    slots = back_ref.shape[0]
    lanes = place_ref.shape[0]
    mover = onehot(place_ref[...] == iota((lanes, slots), 1))
    picked = dot(mover, back_ref[...]).astype(BF16)
    for b in range(w_ref.shape[0]):
        rows = slice(b * n, (b + 1) * n)
        term = dot(w_ref[b], picked[b * k : (b + 1) * k, :])
        out_ref[rows, :] = (solved_ref[rows, :].astype(F32) - term).astype(BF16)


def cost(flops, size):
    return pl.CostEstimate(flops=flops, bytes_accessed=size, transcendentals=0)


def shards(
    rhs_interior,
    rhs_interface,
    inv_blocks,
    coupling,
    interface_map,
    slot_counts,
    column_order,
    schur_inverse,
):
    f32, bf16 = F32, BF16
    nb, n = inv_blocks.shape[:2]
    k = coupling.shape[2]
    cols = rhs_interior.shape[1]
    owners = lax.axis_size(ALL)
    devs = lax.axis_size(DEV)
    secs = lax.axis_size(SEC)
    pairs = owners // 2
    slots = nb * k
    per_pair = slots // pairs
    half = per_pair // 2
    piece = rhs_interface.shape[0]
    pair_rows = 2 * piece
    band = piece * secs
    steps = nb // GROUP
    lanes = GROUP * k

    live = jnp.arange(k, dtype=jnp.int32)[None, :] < slot_counts[:, None]
    marked = jnp.where(live, interface_map, interface_map + DEAD).reshape(steps, 1, lanes)
    block_specs = [
        pl.BlockSpec((GROUP * n, cols), lambda i: (i, 0)),
        pl.BlockSpec((GROUP, n, n), lambda i: (i, 0, 0)),
    ]
    sent, place = pl.pallas_call(
        functools.partial(forward_kernel, (per_pair, half, pair_rows, pairs, devs)),
        grid=(steps,),
        in_specs=[
            pl.BlockSpec((1, 1, lanes), lambda i: (i, 0, 0)),
            *block_specs,
            pl.BlockSpec((GROUP, None, k, n), lambda i: (i, 0, 0, 0)),
        ],
        out_specs=[
            pl.BlockSpec((owners * WIRE, cols), lambda i: (0, 0)),
            pl.BlockSpec((1, 1, lanes), lambda i: (i, 0, 0)),
        ],
        out_shape=[
            jax.ShapeDtypeStruct((owners * WIRE, cols), bf16),
            jax.ShapeDtypeStruct((steps, 1, lanes), f32),
        ],
        scratch_shapes=[pltpu.VMEM((pairs, 128), f32), pltpu.VMEM((pairs, 256), f32)],
        cost_estimate=cost(6 * 10**9, 14 * 10**6),
        name="forward",
    )(marked, rhs_interior, inv_blocks, coupling)
    got = exchange(sent.reshape(owners, WIRE, cols), ALL)
    solved, weights = pl.pallas_call(
        middle_kernel,
        grid=(steps,),
        in_specs=[*block_specs, pl.BlockSpec((GROUP, None, k, n), lambda i: (i, 1, 0, 0))],
        out_specs=[
            pl.BlockSpec((GROUP * n, cols), lambda i: (i, 0)),
            pl.BlockSpec((GROUP, n, k), lambda i: (i, 0, 0)),
        ],
        out_shape=[
            jax.ShapeDtypeStruct((nb * n, cols), bf16),
            jax.ShapeDtypeStruct((nb, n, k), bf16),
        ],
        cost_estimate=cost(2 * 10**9, 20 * 10**6),
        name="middle",
    )(rhs_interior, inv_blocks, coupling)

    core = lax.axis_index("c")
    offs = jnp.where(core == 0, got[:, half, :half], got[:, half, half : 2 * half])
    target = jnp.pad(offs, ((0, 0), (0, WIRE - half)), constant_values=-1.0).reshape(1, -1)
    selector = jnp.arange(pair_rows, dtype=jnp.int32)[:, None].astype(bf16) == target
    arrived = jnp.dot(
        selector.astype(bf16), got.reshape(-1, cols), preferred_element_type=f32
    ).reshape(2, piece, cols)
    rhs_cols = jnp.take(rhs_interface, column_order, axis=1)
    mine = jnp.arange(2)[:, None, None] == core
    own = jnp.where(mine, rhs_cols[None], 0.0) - arrived
    reduced = own + lax.ppermute(own, "c", [(0, 1), (1, 0)])
    reduced = reduced.reshape(pair_rows, cols).astype(bf16)
    section = copies(reduced, "z").reshape(-1, cols)

    product = jnp.dot(schur_inverse, section, preferred_element_type=f32)
    parts = exchange(product.astype(bf16).reshape(secs, piece, cols), SEC)
    summed = jnp.sum(parts.astype(f32), axis=0).astype(bf16)
    values = copies(summed, SEC).reshape(band, cols)

    s = lax.axis_index(SEC)
    asked = lax.dynamic_slice_in_dim(got[:, half + 1 : half + 3], s * devs, devs, axis=0)
    asked = asked.reshape(devs, band // pair_rows, 64)[:, :, :per_pair]
    picker = asked[:, :, :, None] == jnp.arange(pair_rows, dtype=jnp.int32).astype(bf16)
    returned = jnp.einsum(
        "vjkr,jrn->vjkn",
        picker.astype(bf16),
        values.reshape(-1, pair_rows, cols),
        preferred_element_type=f32,
    ).astype(bf16)
    back = exchange(returned.reshape(devs, -1, cols), DEV).reshape(slots, cols)

    interior = pl.pallas_call(
        tail_kernel,
        grid=(steps,),
        in_specs=[
            pl.BlockSpec((lanes, 1), lambda i: (i, 0)),
            pl.BlockSpec((slots, cols), lambda i: (0, 0)),
            pl.BlockSpec((GROUP * n, cols), lambda i: (i, 0)),
            pl.BlockSpec((GROUP, n, k), lambda i: (i, 0, 0)),
        ],
        out_specs=pl.BlockSpec((GROUP * n, cols), lambda i: (i, 0)),
        out_shape=jax.ShapeDtypeStruct((nb * n, cols), bf16),
        cost_estimate=cost(4 * 10**9, 14 * 10**6),
        name="tail",
    )(place.reshape(slots, 1), back, solved, weights)
    return interior, values.astype(f32)


def solution(mesh):
    fine = Mesh(mesh.devices.reshape(4, 4, 4, 2), ALL)
    placed = (
        P(ALL, None),
        P(ALL, None),
        P(ALL, None, None),
        P(ALL, None, None, None),
        P(ALL, None),
        P(ALL),
        P(),
        P(DEV, SEC),
    )
    return jax.shard_map(
        shards,
        mesh=fine,
        in_specs=placed,
        out_specs=(P(ALL, None), P(DEV, None)),
        check_vma=False,
    )
```

```python
import functools

import jax
import jax.numpy as jnp
from jax import lax
from jax.experimental import pallas as pl
from jax.experimental.pallas import tpu as pltpu
from jax.sharding import Mesh
from jax.sharding import PartitionSpec as P

ALL = ("y", "x", "z", "c")
SEC = ("y", "x")
DEV = ("z", "c")
WIRE = 24
GROUP = 4
F32, BF16 = jnp.float32, jnp.bfloat16


def exchange(blocks, axis):
    return lax.all_to_all(blocks, axis, 0, 0, tiled=True)


def copies(array, axis):
    size = lax.axis_size(axis)
    return exchange(jnp.broadcast_to(array[None], (size, *array.shape)), axis)


def iota(shape, dim):
    return lax.broadcasted_iota(jnp.int32, shape, dim).astype(F32)


def quotient(x, n):
    return jnp.floor((x + 0.5) * (1.0 / n))


def dot(a, b, dims=((1,), (0,))):
    return lax.dot_general(a, b, (dims, ((), ())), preferred_element_type=F32)


def onehot(mask):
    return jnp.where(mask, 1.0, 0.0).astype(BF16)


def rank_kernel(sizes, counts_ref, map_ref, wire_ref, place_ref, index_ref):
    per_pair, half, pair_rows, pairs, owners = sizes
    blocks, k = map_ref.shape
    lanes = GROUP * k
    upper = onehot(iota((lanes, lanes), 0) < iota((lanes, lanes), 1))
    row64 = (lax.broadcasted_iota(jnp.int32, (256, lanes), 0) & 63).astype(F32)
    lane = lax.broadcasted_iota(jnp.int32, (1, k), 1)
    wire_ref[0:1, :] = jnp.full((1, lanes), owners * WIRE, jnp.int32)
    place_ref[blocks // GROUP :, :] = jnp.full((1, lanes), pairs * per_pair, jnp.int32)
    base = jnp.zeros((pairs, 1), F32)
    offs = jnp.zeros((pairs, 256), F32)
    for g in range(blocks // GROUP):
        mine = range(g * GROUP, (g + 1) * GROUP)
        slot = jnp.concatenate([map_ref[b : b + 1, :] for b in mine], axis=1).astype(F32)
        live = jnp.concatenate(
            [jnp.where(lane < counts_ref[b], 1.0, 0.0) for b in mine], axis=1
        )
        dead = live == 0.0
        pair = quotient(slot, pair_rows)
        off = slot - pair_rows * pair
        table = jnp.where(iota((pairs, lanes), 0) == pair, 1.0, 0.0)
        before = dot(table.astype(BF16), upper)
        rank = jnp.sum(table * (before + base), axis=0, keepdims=True)
        base = base + jnp.sum(table, axis=1, keepdims=True)
        place = pair * per_pair + rank
        wire = place + (WIRE - half) * quotient(place, half)
        place_ref[g : g + 1, :] = jnp.where(dead, pairs * per_pair, place).astype(jnp.int32)
        wire_ref[g + 1 : g + 2, :] = jnp.where(dead, owners * WIRE, wire).astype(jnp.int32)
        offs = offs + dot((table * off).astype(BF16), onehot(row64 == rank), ((1,), (1,)))
    p = lax.broadcasted_iota(jnp.int32, offs.shape, 0)
    at = lax.broadcasted_iota(jnp.int32, offs.shape, 1)
    spread = jnp.where((at >> 6) == (p & 3), offs, 0.0).astype(BF16)
    groups = pairs // 4
    member = iota((groups, pairs), 0) == quotient(iota((groups, pairs), 1), 4)
    index_ref[:pairs, :] = offs
    index_ref[pairs:, :] = dot(onehot(member), spread)


def forward_kernel(
    sizes, wire_ref, index_ref, rhs_ref, inv_ref, couple_ref, out_ref, wide_ref, stage_ref
):
    half, pairs, devs = sizes
    step = pl.program_id(0)
    n = inv_ref.shape[1]
    k = couple_ref.shape[1]
    lanes = GROUP * k
    rows_out = out_ref.shape[0]

    @pl.when(step == 0)
    def _():
        wide_ref[...] = jnp.zeros_like(wide_ref)
        stage_ref[...] = jnp.zeros_like(stage_ref)
        for d in range(rows_out // WIRE):
            v = d % devs
            for r, m in enumerate((d // 2, pairs + 2 * v, pairs + 2 * v + 1)):
                w = d * WIRE + half + r
                wide_ref[0, w : w + 1, :] = index_ref[m : m + 1, :128]
                wide_ref[1, w : w + 1, :] = index_ref[m : m + 1, 128:]

    def move(step, first, last):
        here = wire_ref.at[pl.ds(step * lanes, lanes)]
        for i in range(first, last):
            row = pl.ds(here[i], 1)
            wide_ref[:, row, :] = stage_ref[:, i : i + 1, :]

    solved = [
        dot(inv_ref[b], rhs_ref[b * n : (b + 1) * n, :]).astype(BF16) for b in range(GROUP)
    ]
    move(step, 0, lanes // 2)
    parts = [dot(couple_ref[b], solved[b]) for b in range(GROUP)]
    move(step, lanes // 2, lanes)
    for b in range(GROUP):
        own = slice(b * k, (b + 1) * k)
        stage_ref[0, own, :] = parts[b][:, :128]
        stage_ref[1, own, :] = parts[b][:, 128:]

    @pl.when(step == pl.num_programs(0) - 1)
    def _():
        move(step + 1, 0, lanes)
        for t in range(rows_out // 256):
            rows = slice(256 * t, 256 * (t + 1))
            out_ref[rows, :128] = wide_ref[0, rows, :].astype(BF16)
            out_ref[rows, 128:] = wide_ref[1, rows, :].astype(BF16)


def middle_kernel(rhs_ref, inv_ref, couple_ref, solved_ref, w_ref):
    n = inv_ref.shape[1]
    for b in range(inv_ref.shape[0]):
        rows = slice(b * n, (b + 1) * n)
        solved_ref[rows, :] = dot(inv_ref[b], rhs_ref[rows, :]).astype(BF16)
        w_ref[b] = dot(inv_ref[b], couple_ref[b], ((1,), (1,))).astype(BF16)


def tail_kernel(place_ref, back_ref, solved_ref, w_ref, out_ref, wide_ref, pick_ref):
    n = w_ref.shape[1]
    k = w_ref.shape[2]
    slots = back_ref.shape[0]
    lanes = GROUP * k
    step = pl.program_id(0)

    def gather(step, first, last):
        here = place_ref.at[pl.ds(step * lanes, lanes)]
        for i in range(first, last):
            row = pl.ds(here[i], 1)
            pick_ref[:, i : i + 1, :] = wide_ref[:, row, :]

    @pl.when(step == 0)
    def _():
        for t in range(slots // 256):
            rows = slice(256 * t, 256 * (t + 1))
            wide_ref[0, rows, :] = back_ref[rows, :128].astype(F32)
            wide_ref[1, rows, :] = back_ref[rows, 128:].astype(F32)
        wide_ref[:, slots:, :] = jnp.zeros_like(wide_ref[:, slots:, :])
        gather(step, 0, lanes)

    picked = jnp.concatenate([pick_ref[0], pick_ref[1]], axis=1).astype(BF16)
    for b in range(GROUP):
        rows = slice(b * n, (b + 1) * n)
        term = dot(w_ref[b], picked[b * k : (b + 1) * k, :])
        gather(step + 1, b * k, (b + 1) * k)
        out_ref[rows, :] = (solved_ref[rows, :].astype(F32) - term).astype(BF16)


def cost(flops, size):
    return pl.CostEstimate(flops=flops, bytes_accessed=size, transcendentals=0)


def shards(
    rhs_interior,
    rhs_interface,
    inv_blocks,
    coupling,
    interface_map,
    slot_counts,
    column_order,
    schur_inverse,
):
    f32, bf16 = F32, BF16
    nb, n = inv_blocks.shape[:2]
    k = coupling.shape[2]
    cols = rhs_interior.shape[1]
    owners = lax.axis_size(ALL)
    devs = lax.axis_size(DEV)
    secs = lax.axis_size(SEC)
    pairs = owners // 2
    slots = nb * k
    per_pair = slots // pairs
    half = per_pair // 2
    piece = rhs_interface.shape[0]
    pair_rows = 2 * piece
    band = piece * secs
    steps = nb // GROUP
    lanes = GROUP * k

    block_specs = [
        pl.BlockSpec((GROUP * n, cols), lambda i: (i, 0)),
        pl.BlockSpec((GROUP, n, n), lambda i: (i, 0, 0)),
    ]
    whole = pl.BlockSpec(memory_space=pltpu.VMEM)
    wire, place, index = pl.pallas_call(
        functools.partial(rank_kernel, (per_pair, half, pair_rows, pairs, owners)),
        in_specs=[pl.BlockSpec(memory_space=pltpu.SMEM), whole],
        out_specs=[whole, whole, whole],
        out_shape=[
            jax.ShapeDtypeStruct((steps + 1, lanes), jnp.int32),
            jax.ShapeDtypeStruct((steps + 1, lanes), jnp.int32),
            jax.ShapeDtypeStruct((pairs + pairs // 4, 256), f32),
        ],
        cost_estimate=cost(10**8, 10**5),
        name="rank",
    )(slot_counts, interface_map)
    sent = pl.pallas_call(
        functools.partial(forward_kernel, (half, pairs, devs)),
        grid_spec=pltpu.PrefetchScalarGridSpec(
            num_scalar_prefetch=1,
            grid=(steps,),
            in_specs=[
                pl.BlockSpec(index.shape, lambda i, at: (0, 0)),
                pl.BlockSpec((GROUP * n, cols), lambda i, at: (i, 0)),
                pl.BlockSpec((GROUP, n, n), lambda i, at: (i, 0, 0)),
                pl.BlockSpec((GROUP, None, k, n), lambda i, at: (i, 0, 0, 0)),
            ],
            out_specs=pl.BlockSpec((owners * WIRE, cols), lambda i, at: (0, 0)),
            scratch_shapes=[
                pltpu.VMEM((2, owners * WIRE + 8, 128), f32),
                pltpu.VMEM((2, lanes, 128), f32),
            ],
        ),
        out_shape=jax.ShapeDtypeStruct((owners * WIRE, cols), bf16),
        cost_estimate=cost(2 * 10**9, 14 * 10**6),
        name="forward",
    )(wire.reshape(-1), index, rhs_interior, inv_blocks, coupling)
    got = exchange(sent.reshape(owners, WIRE, cols), ALL)
    solved, weights = pl.pallas_call(
        middle_kernel,
        grid=(steps,),
        in_specs=[*block_specs, pl.BlockSpec((GROUP, None, k, n), lambda i: (i, 1, 0, 0))],
        out_specs=[
            pl.BlockSpec((GROUP * n, cols), lambda i: (i, 0)),
            pl.BlockSpec((GROUP, n, k), lambda i: (i, 0, 0)),
        ],
        out_shape=[
            jax.ShapeDtypeStruct((nb * n, cols), bf16),
            jax.ShapeDtypeStruct((nb, n, k), bf16),
        ],
        cost_estimate=cost(2 * 10**9, 20 * 10**6),
        name="middle",
    )(rhs_interior, inv_blocks, coupling)

    core = lax.axis_index("c")
    offs = jnp.where(core == 0, got[:, half, :half], got[:, half, half : 2 * half])
    target = jnp.pad(offs, ((0, 0), (0, WIRE - half)), constant_values=-1.0).reshape(1, -1)
    selector = jnp.arange(pair_rows, dtype=jnp.int32)[:, None].astype(bf16) == target
    arrived = jnp.dot(
        selector.astype(bf16), got.reshape(-1, cols), preferred_element_type=f32
    ).reshape(2, piece, cols)
    rhs_cols = jnp.take(rhs_interface, column_order, axis=1)
    mine = jnp.arange(2)[:, None, None] == core
    own = jnp.where(mine, rhs_cols[None], 0.0) - arrived
    reduced = own + lax.ppermute(own, "c", [(0, 1), (1, 0)])
    reduced = reduced.reshape(pair_rows, cols).astype(bf16)
    section = copies(reduced, "z").reshape(-1, cols)

    product = jnp.dot(schur_inverse, section, preferred_element_type=f32)
    parts = exchange(product.astype(bf16).reshape(secs, piece, cols), SEC)
    summed = jnp.sum(parts.astype(f32), axis=0).astype(bf16)
    values = copies(summed, SEC).reshape(band, cols)

    s = lax.axis_index(SEC)
    asked = lax.dynamic_slice_in_dim(got[:, half + 1 : half + 3], s * devs, devs, axis=0)
    asked = asked.reshape(devs, band // pair_rows, 64)[:, :, :per_pair]
    picker = asked[:, :, :, None] == jnp.arange(pair_rows, dtype=jnp.int32).astype(bf16)
    returned = jnp.einsum(
        "vjkr,jrn->vjkn",
        picker.astype(bf16),
        values.reshape(-1, pair_rows, cols),
        preferred_element_type=f32,
    ).astype(bf16)
    back = exchange(returned.reshape(devs, -1, cols), DEV).reshape(slots, cols)

    interior = pl.pallas_call(
        tail_kernel,
        grid_spec=pltpu.PrefetchScalarGridSpec(
            num_scalar_prefetch=1,
            grid=(steps,),
            in_specs=[
                pl.BlockSpec((slots, cols), lambda i, at: (0, 0)),
                pl.BlockSpec((GROUP * n, cols), lambda i, at: (i, 0)),
                pl.BlockSpec((GROUP, n, k), lambda i, at: (i, 0, 0)),
            ],
            out_specs=pl.BlockSpec((GROUP * n, cols), lambda i, at: (i, 0)),
            scratch_shapes=[
                pltpu.VMEM((2, slots + 8, 128), f32),
                pltpu.VMEM((2, lanes, 128), f32),
            ],
        ),
        out_shape=jax.ShapeDtypeStruct((nb * n, cols), bf16),
        cost_estimate=cost(4 * 10**9, 14 * 10**6),
        name="tail",
    )(place.reshape(-1), back, solved, weights)
    return interior, values.astype(f32)


def solution(mesh):
    fine = Mesh(mesh.devices.reshape(4, 4, 4, 2), ALL)
    placed = (
        P(ALL, None),
        P(ALL, None),
        P(ALL, None, None),
        P(ALL, None, None, None),
        P(ALL, None),
        P(ALL),
        P(),
        P(DEV, SEC),
    )
    return jax.shard_map(
        shards,
        mesh=fine,
        in_specs=placed,
        out_specs=(P(ALL, None), P(DEV, None)),
        check_vma=False,
    )
```

```python
import functools

import jax
import jax.numpy as jnp
from jax import lax
from jax.experimental import pallas as pl
from jax.experimental.pallas import tpu as pltpu
from jax.sharding import Mesh
from jax.sharding import PartitionSpec as P

ALL = ("y", "x", "z", "c")
SEC = ("y", "x")
DEV = ("z", "c")
WIRE = 24
GROUP = 4
F32, BF16 = jnp.float32, jnp.bfloat16


def exchange(blocks, axis):
    return lax.all_to_all(blocks, axis, 0, 0, tiled=True)


def copies(array, axis):
    size = lax.axis_size(axis)
    return exchange(jnp.broadcast_to(array[None], (size, *array.shape)), axis)


def iota(shape, dim):
    return lax.broadcasted_iota(jnp.int32, shape, dim).astype(F32)


def quotient(x, n):
    return jnp.floor((x + 0.5) * (1.0 / n))


def dot(a, b, dims=((1,), (0,))):
    return lax.dot_general(a, b, (dims, ((), ())), preferred_element_type=F32)


def onehot(mask):
    return jnp.where(mask, 1.0, 0.0).astype(BF16)


def forward_kernel(
    sizes, counts_ref, map_ref, rhs_ref, inv_ref, couple_ref, out_ref, place_ref,
    wide_ref, stage_ref, base_ref, offs_ref, wire_ref, at_ref, sem
):
    per_pair, half, pair_rows, pairs, devs = sizes
    step = pl.program_id(0)
    n = inv_ref.shape[1]
    k = couple_ref.shape[1]
    lanes = GROUP * k
    rows_out = out_ref.shape[0]
    now, before = lax.rem(step, 2), lax.rem(step + 1, 2)

    def handover(slot):
        return pltpu.make_async_copy(wire_ref.at[slot], at_ref.at[slot], sem.at[slot])

    @pl.when(step == 0)
    def _():
        stage_ref[...] = jnp.zeros_like(stage_ref)
        base_ref[...] = jnp.zeros_like(base_ref)
        offs_ref[...] = jnp.zeros_like(offs_ref)
        for i in range(lanes):
            at_ref[1, 0, i] = rows_out

    @pl.when(step > 0)
    def _():
        handover(before).wait()

    slot = jnp.concatenate(
        [map_ref[pl.ds(step * GROUP + b, 1), :] for b in range(GROUP)], axis=1
    ).astype(F32)
    at = lax.broadcasted_iota(jnp.int32, (1, k), 1)
    live = jnp.concatenate(
        [jnp.where(at < counts_ref[step * GROUP + b], 1.0, 0.0) for b in range(GROUP)], axis=1
    )
    pair = quotient(slot, pair_rows)
    off = slot - pair_rows * pair
    table = jnp.where(iota((pairs, lanes), 0) == pair, 1.0, 0.0)
    earlier = dot(
        table.astype(BF16), onehot(iota((lanes, lanes), 0) < iota((lanes, lanes), 1))
    )
    rank = jnp.sum(table * (earlier + base_ref[:, :1]), axis=0, keepdims=True)
    base_ref[...] += jnp.sum(table, axis=1, keepdims=True)
    place = pair * per_pair + rank
    place_ref[0] = jnp.where(live == 0.0, pairs * per_pair, place).astype(jnp.int32)
    wire = place + (WIRE - half) * quotient(place, half)
    wire_ref[now] = wire.astype(jnp.int32)
    handover(now).start()
    row64 = (lax.broadcasted_iota(jnp.int32, (256, lanes), 0) & 63).astype(F32)
    offs_ref[...] += dot((table * off).astype(BF16), onehot(row64 == rank), ((1,), (1,)))

    def move(slot, first, last):
        for i in range(first, last):
            row = pl.ds(at_ref[slot, 0, i], 1)
            wide_ref[:, row, :] = stage_ref[:, i : i + 1, :]

    solved = [
        dot(inv_ref[b], rhs_ref[b * n : (b + 1) * n, :]).astype(BF16) for b in range(GROUP)
    ]
    move(before, 0, lanes // 2)
    parts = [dot(couple_ref[b], solved[b]) for b in range(GROUP)]
    move(before, lanes // 2, lanes)
    depth = lax.broadcasted_iota(jnp.int32, (k, 2 * 128), 0)
    for b in range(GROUP):
        own = slice(b * k, (b + 1) * k)
        part = jnp.where(depth < counts_ref[step * GROUP + b], parts[b], 0.0)
        stage_ref[0, own, :] = part[:, :128]
        stage_ref[1, own, :] = part[:, 128:]

    @pl.when(step == pl.num_programs(0) - 1)
    def _():
        handover(now).wait()
        move(now, 0, lanes)
        offs = offs_ref[...]
        p = lax.broadcasted_iota(jnp.int32, offs.shape, 0)
        lane = lax.broadcasted_iota(jnp.int32, offs.shape, 1)
        spread = jnp.where((lane >> 6) == (p & 3), offs, 0.0).astype(BF16)
        groups = pairs // 4
        member = iota((groups, pairs), 0) == quotient(iota((groups, pairs), 1), 4)
        wanted = dot(onehot(member), spread)
        level = lax.broadcasted_iota(jnp.int32, (WIRE - half, 128), 0)
        for h in range(2):
            cut = slice(128 * h, 128 * (h + 1))
            for v in range(devs):
                one = jnp.broadcast_to(wanted[2 * v : 2 * v + 1, cut], level.shape)
                two = jnp.broadcast_to(wanted[2 * v + 1 : 2 * v + 2, cut], level.shape)
                tail = jnp.where(level == 1, one, jnp.where(level == 2, two, 0.0))
                for d in range(v, rows_out // WIRE, devs):
                    own = jnp.broadcast_to(offs_ref[d // 2 : d // 2 + 1, cut], level.shape)
                    w = d * WIRE + half
                    wide_ref[h, w : w + WIRE - half, :] = jnp.where(level == 0, own, tail)
        for t in range(rows_out // 256):
            rows = slice(256 * t, 256 * (t + 1))
            out_ref[rows, :128] = wide_ref[0, rows, :].astype(BF16)
            out_ref[rows, 128:] = wide_ref[1, rows, :].astype(BF16)


def middle_kernel(rhs_ref, inv_ref, couple_ref, solved_ref, w_ref):
    n = inv_ref.shape[1]
    for b in range(GROUP):
        rows = slice(b * n, (b + 1) * n)
        solved_ref[rows, :] = dot(inv_ref[b], rhs_ref[rows, :]).astype(BF16)
    for b in range(0, GROUP, 2):
        w_ref[b // 2] = jnp.concatenate(
            [dot(inv_ref[c], couple_ref[c], ((1,), (1,))) for c in (b, b + 1)], axis=1
        ).astype(BF16)


def tail_kernel(place_ref, back_ref, solved_ref, w_ref, out_ref, wide_ref, pick_ref):
    n = w_ref.shape[1]
    k = w_ref.shape[2] // 2
    slots = back_ref.shape[0]
    lanes = GROUP * k
    step = pl.program_id(0)

    def gather(step, first, last):
        here = place_ref.at[pl.ds(step * lanes, lanes)]
        for i in range(first, last):
            row = pl.ds(here[i], 1)
            pick_ref[:, i : i + 1, :] = wide_ref[:, row, :]

    @pl.when(step == 0)
    def _():
        for t in range(slots // 256):
            rows = slice(256 * t, 256 * (t + 1))
            wide_ref[0, rows, :] = back_ref[rows, :128].astype(F32)
            wide_ref[1, rows, :] = back_ref[rows, 128:].astype(F32)
        wide_ref[:, slots:, :] = jnp.zeros_like(wide_ref[:, slots:, :])
        gather(step, 0, lanes)

    picked = jnp.concatenate([pick_ref[0], pick_ref[1]], axis=1).astype(BF16)
    empty = jnp.zeros((k, picked.shape[1]), BF16)
    for b in range(GROUP):
        rows = slice(b * n, (b + 1) * n)
        own = picked[b * k : (b + 1) * k, :]
        pad = [own, empty] if b % 2 == 0 else [empty, own]
        term = dot(w_ref[b // 2], jnp.concatenate(pad, axis=0))
        gather(step + 1, b * k, (b + 1) * k)
        out_ref[rows, :] = (solved_ref[rows, :].astype(F32) - term).astype(BF16)


def cost(flops, size):
    return pl.CostEstimate(flops=flops, bytes_accessed=size, transcendentals=0)


def shards(
    rhs_interior,
    rhs_interface,
    inv_blocks,
    coupling,
    interface_map,
    slot_counts,
    column_order,
    schur_inverse,
):
    f32, bf16 = F32, BF16
    nb, n = inv_blocks.shape[:2]
    k = coupling.shape[2]
    cols = rhs_interior.shape[1]
    owners = lax.axis_size(ALL)
    devs = lax.axis_size(DEV)
    secs = lax.axis_size(SEC)
    pairs = owners // 2
    slots = nb * k
    per_pair = slots // pairs
    half = per_pair // 2
    piece = rhs_interface.shape[0]
    pair_rows = 2 * piece
    band = piece * secs
    steps = nb // GROUP
    lanes = GROUP * k

    block_specs = [
        pl.BlockSpec((GROUP * n, cols), lambda i: (i, 0)),
        pl.BlockSpec((GROUP, n, n), lambda i: (i, 0, 0)),
    ]
    sent, place = pl.pallas_call(
        functools.partial(forward_kernel, (per_pair, half, pair_rows, pairs, devs)),
        grid_spec=pltpu.PrefetchScalarGridSpec(
            num_scalar_prefetch=1,
            grid=(steps,),
            in_specs=[
                pl.BlockSpec((nb, k), lambda i, at: (0, 0)),
                pl.BlockSpec((GROUP * n, cols), lambda i, at: (i, 0)),
                pl.BlockSpec((GROUP, n, n), lambda i, at: (i, 0, 0)),
                pl.BlockSpec((GROUP, None, k, n), lambda i, at: (i, 0, 0, 0)),
            ],
            out_specs=[
                pl.BlockSpec((owners * WIRE, cols), lambda i, at: (0, 0)),
                pl.BlockSpec((1, 1, lanes), lambda i, at: (i, 0, 0)),
            ],
            scratch_shapes=[
                pltpu.VMEM((2, owners * WIRE + 8, 128), f32),
                pltpu.VMEM((2, lanes, 128), f32),
                pltpu.VMEM((pairs, 128), f32),
                pltpu.VMEM((pairs, 256), f32),
                pltpu.VMEM((2, 1, lanes), jnp.int32),
                pltpu.SMEM((2, 1, lanes), jnp.int32),
                pltpu.SemaphoreType.DMA((2,)),
            ],
        ),
        out_shape=[
            jax.ShapeDtypeStruct((owners * WIRE, cols), bf16),
            jax.ShapeDtypeStruct((steps, 1, lanes), jnp.int32),
        ],
        cost_estimate=cost(2 * 10**9, 14 * 10**6),
        name="forward",
    )(slot_counts, interface_map, rhs_interior, inv_blocks, coupling)
    got = exchange(sent.reshape(owners, WIRE, cols), ALL)
    solved, weights = pl.pallas_call(
        middle_kernel,
        grid=(steps,),
        in_specs=[*block_specs, pl.BlockSpec((GROUP, None, k, n), lambda i: (i, 1, 0, 0))],
        out_specs=[
            pl.BlockSpec((GROUP * n, cols), lambda i: (i, 0)),
            pl.BlockSpec((GROUP // 2, n, 2 * k), lambda i: (i, 0, 0)),
        ],
        out_shape=[
            jax.ShapeDtypeStruct((nb * n, cols), bf16),
            jax.ShapeDtypeStruct((nb // 2, n, 2 * k), bf16),
        ],
        cost_estimate=cost(2 * 10**9, 20 * 10**6),
        name="middle",
    )(rhs_interior, inv_blocks, coupling)

    core = lax.axis_index("c")
    offs = jnp.where(core == 0, got[:, half, :half], got[:, half, half : 2 * half])
    offs, solved, weights = lax.optimization_barrier((offs, solved, weights))
    target = jnp.pad(offs, ((0, 0), (0, WIRE - half)), constant_values=-1.0).reshape(1, -1)
    selector = jnp.arange(pair_rows, dtype=jnp.int32)[:, None].astype(bf16) == target
    arrived = jnp.dot(
        selector.astype(bf16), got.reshape(-1, cols), preferred_element_type=f32
    ).reshape(2, piece, cols)
    rhs_cols = jnp.take(rhs_interface, column_order, axis=1)
    mine = jnp.arange(2)[:, None, None] == core
    own = jnp.where(mine, rhs_cols[None], 0.0) - arrived
    reduced = own + lax.ppermute(own, "c", [(0, 1), (1, 0)])
    reduced = reduced.reshape(pair_rows, cols).astype(bf16)
    section = copies(reduced, "z").reshape(-1, cols)

    product = jnp.dot(schur_inverse, section, preferred_element_type=f32)
    parts = exchange(product.astype(bf16).reshape(secs, piece, cols), SEC)
    summed = jnp.sum(parts.astype(f32), axis=0).astype(bf16)
    values = copies(summed, SEC).reshape(band, cols)

    s = lax.axis_index(SEC)
    asked = lax.dynamic_slice_in_dim(got[:, half + 1 : half + 3], s * devs, devs, axis=0)
    asked = asked.reshape(devs, band // pair_rows, 64)[:, :, :per_pair]
    picker = asked[:, :, :, None] == jnp.arange(pair_rows, dtype=jnp.int32).astype(bf16)
    returned = jnp.einsum(
        "vjkr,jrn->vjkn",
        picker.astype(bf16),
        values.reshape(-1, pair_rows, cols),
        preferred_element_type=f32,
    ).astype(bf16)
    back = exchange(returned.reshape(devs, -1, cols), DEV).reshape(slots, cols)

    interior = pl.pallas_call(
        tail_kernel,
        grid_spec=pltpu.PrefetchScalarGridSpec(
            num_scalar_prefetch=1,
            grid=(steps,),
            in_specs=[
                pl.BlockSpec((slots, cols), lambda i, at: (0, 0)),
                pl.BlockSpec((GROUP * n, cols), lambda i, at: (i, 0)),
                pl.BlockSpec((GROUP // 2, n, 2 * k), lambda i, at: (i, 0, 0)),
            ],
            out_specs=pl.BlockSpec((GROUP * n, cols), lambda i, at: (i, 0)),
            scratch_shapes=[
                pltpu.VMEM((2, slots + 8, 128), f32),
                pltpu.VMEM((2, lanes, 128), f32),
            ],
        ),
        out_shape=jax.ShapeDtypeStruct((nb * n, cols), bf16),
        cost_estimate=cost(4 * 10**9, 14 * 10**6),
        name="tail",
    )(jnp.pad(place.reshape(-1), (0, lanes), constant_values=slots), back, solved, weights)
    return interior, values.astype(f32)


def solution(mesh):
    fine = Mesh(mesh.devices.reshape(4, 4, 4, 2), ALL)
    placed = (
        P(ALL, None),
        P(ALL, None),
        P(ALL, None, None),
        P(ALL, None, None, None),
        P(ALL, None),
        P(ALL),
        P(),
        P(DEV, SEC),
    )
    return jax.shard_map(
        shards,
        mesh=fine,
        in_specs=placed,
        out_specs=(P(ALL, None), P(DEV, None)),
        check_vma=False,
    )
```

```python
import functools

import jax
import jax.numpy as jnp
from jax import lax
from jax.experimental import pallas as pl
from jax.experimental.pallas import tpu as pltpu
from jax.sharding import Mesh
from jax.sharding import PartitionSpec as P

ALL = ("y", "x", "z", "c")
SEC = ("y", "x")
DEV = ("z", "c")
WIRE = 24
GROUP = 4
F32, BF16 = jnp.float32, jnp.bfloat16


def exchange(blocks, axis):
    return lax.all_to_all(blocks, axis, 0, 0, tiled=True)


def copies(array, axis):
    size = lax.axis_size(axis)
    return exchange(jnp.broadcast_to(array[None], (size, *array.shape)), axis)


def iota(shape, dim):
    return lax.broadcasted_iota(jnp.int32, shape, dim).astype(F32)


def quotient(x, n):
    return jnp.floor((x + 0.5) * (1.0 / n))


def dot(a, b, dims=((1,), (0,))):
    return lax.dot_general(a, b, (dims, ((), ())), preferred_element_type=F32)


def onehot(mask):
    return jnp.where(mask, 1.0, 0.0).astype(BF16)


def forward_kernel(
    sizes, counts_ref, map_ref, rhs_ref, inv_ref, couple_ref, out_ref, place_ref,
    wide_ref, stage_ref, base_ref, offs_ref, wire_ref, at_ref, sem
):
    per_pair, half, pair_rows, pairs, devs = sizes
    step = pl.program_id(0)
    n = inv_ref.shape[1]
    k = couple_ref.shape[1]
    lanes = GROUP * k
    rows_out = out_ref.shape[0]
    now, before = lax.rem(step, 2), lax.rem(step + 1, 2)

    def handover(slot):
        return pltpu.make_async_copy(wire_ref.at[slot], at_ref.at[slot], sem.at[slot])

    @pl.when(step == 0)
    def _():
        stage_ref[...] = jnp.zeros_like(stage_ref)
        base_ref[...] = jnp.zeros_like(base_ref)
        offs_ref[...] = jnp.zeros_like(offs_ref)
        for i in range(lanes):
            at_ref[1, 0, i] = 2 * rows_out

    @pl.when(step > 0)
    def _():
        handover(before).wait()

    slot = jnp.concatenate(
        [map_ref[pl.ds(step * GROUP + b, 1), :] for b in range(GROUP)], axis=1
    ).astype(F32)
    at = lax.broadcasted_iota(jnp.int32, (1, k), 1)
    live = jnp.concatenate(
        [jnp.where(at < counts_ref[step * GROUP + b], 1.0, 0.0) for b in range(GROUP)], axis=1
    )
    pair = quotient(slot, pair_rows)
    off = slot - pair_rows * pair
    table = jnp.where(iota((pairs, lanes), 0) == pair, 1.0, 0.0)
    earlier = dot(
        table.astype(BF16), onehot(iota((lanes, lanes), 0) < iota((lanes, lanes), 1))
    )
    rank = jnp.sum(table * (earlier + base_ref[:, :1]), axis=0, keepdims=True)
    base_ref[...] += jnp.sum(table, axis=1, keepdims=True)
    place = pair * per_pair + rank
    place_ref[0] = (2.0 * jnp.where(live == 0.0, pairs * per_pair, place)).astype(jnp.int32)
    wire = place + (WIRE - half) * quotient(place, half)
    wire_ref[now] = (2.0 * wire).astype(jnp.int32)
    handover(now).start()
    row64 = (lax.broadcasted_iota(jnp.int32, (256, lanes), 0) & 63).astype(F32)
    offs_ref[...] += dot((table * off).astype(BF16), onehot(row64 == rank), ((1,), (1,)))

    def move(slot, first, last):
        for i in range(first, last):
            row = pl.ds(pl.multiple_of(at_ref[slot, 0, i], 2), 2)
            wide_ref[row, :] = stage_ref[2 * i : 2 * i + 2, :]

    solved = [
        dot(inv_ref[b], rhs_ref[b * n : (b + 1) * n, :]).astype(BF16) for b in range(GROUP)
    ]
    move(before, 0, lanes // 2)
    parts = [dot(couple_ref[b], solved[b]) for b in range(GROUP)]
    move(before, lanes // 2, lanes)
    depth = lax.broadcasted_iota(jnp.int32, (k, 2 * 128), 0)
    for b in range(GROUP):
        part = jnp.where(depth < counts_ref[step * GROUP + b], parts[b], 0.0)
        stage_ref[pl.ds(2 * b * k, k, stride=2), :] = part[:, :128]
        stage_ref[pl.ds(2 * b * k + 1, k, stride=2), :] = part[:, 128:]

    @pl.when(step == pl.num_programs(0) - 1)
    def _():
        handover(now).wait()
        move(now, 0, lanes)
        offs = offs_ref[...]
        p = lax.broadcasted_iota(jnp.int32, offs.shape, 0)
        lane = lax.broadcasted_iota(jnp.int32, offs.shape, 1)
        spread = jnp.where((lane >> 6) == (p & 3), offs, 0.0).astype(BF16)
        groups = pairs // 4
        member = iota((groups, pairs), 0) == quotient(iota((groups, pairs), 1), 4)
        wanted = dot(onehot(member), spread)
        level = lax.broadcasted_iota(jnp.int32, (2 * (WIRE - half), 128), 0)

        def spread_rows(parts, rest):
            for at, part in parts:
                rest = jnp.where(level == at, jnp.broadcast_to(part, level.shape), rest)
            return rest

        for v in range(devs):
            rows = [wanted[2 * v + r : 2 * v + r + 1, :] for r in range(2)]
            fixed = spread_rows(
                [(2 + 2 * r + h, rows[r][:, 128 * h : 128 * (h + 1)]) for r in range(2) for h in range(2)],
                jnp.zeros(level.shape, F32),
            )
            for d in range(v, rows_out // WIRE, devs):
                own = [(h, offs_ref[d // 2 : d // 2 + 1, 128 * h : 128 * (h + 1)]) for h in range(2)]
                w = 2 * (d * WIRE + half)
                wide_ref[w : w + 2 * (WIRE - half), :] = spread_rows(own, fixed)
        for t in range(rows_out // 256):
            rows = slice(256 * t, 256 * (t + 1))
            for h in range(2):
                out_ref[rows, 128 * h : 128 * (h + 1)] = wide_ref[
                    pl.ds(512 * t + h, 256, stride=2), :
                ].astype(BF16)


def middle_kernel(rhs_ref, inv_ref, couple_ref, solved_ref, w_ref):
    n = inv_ref.shape[1]
    for b in range(GROUP):
        rows = slice(b * n, (b + 1) * n)
        solved_ref[rows, :] = dot(inv_ref[b], rhs_ref[rows, :]).astype(BF16)
    for b in range(0, GROUP, 2):
        w_ref[b // 2] = jnp.concatenate(
            [dot(inv_ref[c], couple_ref[c], ((1,), (1,))) for c in (b, b + 1)], axis=1
        ).astype(BF16)


def tail_kernel(place_ref, back_ref, solved_ref, w_ref, out_ref, wide_ref, pick_ref):
    n = w_ref.shape[1]
    k = w_ref.shape[2] // 2
    slots = back_ref.shape[0]
    lanes = GROUP * k
    step = pl.program_id(0)

    def gather(step, first, last):
        here = place_ref.at[pl.ds(step * lanes, lanes)]
        for i in range(first, last):
            row = pl.ds(pl.multiple_of(here[i], 2), 2)
            pick_ref[2 * i : 2 * i + 2, :] = wide_ref[row, :]

    @pl.when(step == 0)
    def _():
        for t in range(slots // 256):
            rows = slice(256 * t, 256 * (t + 1))
            for h in range(2):
                wide_ref[pl.ds(512 * t + h, 256, stride=2), :] = back_ref[
                    rows, 128 * h : 128 * (h + 1)
                ].astype(F32)
        wide_ref[2 * slots :, :] = jnp.zeros_like(wide_ref[2 * slots :, :])
        gather(step, 0, lanes)

    picked = jnp.concatenate(
        [pick_ref[pl.ds(h, lanes, stride=2), :] for h in range(2)], axis=1
    ).astype(BF16)
    empty = jnp.zeros((k, picked.shape[1]), BF16)
    for b in range(GROUP):
        rows = slice(b * n, (b + 1) * n)
        own = picked[b * k : (b + 1) * k, :]
        pad = [own, empty] if b % 2 == 0 else [empty, own]
        term = dot(w_ref[b // 2], jnp.concatenate(pad, axis=0))
        gather(step + 1, b * k, (b + 1) * k)
        out_ref[rows, :] = (solved_ref[rows, :].astype(F32) - term).astype(BF16)


def cost(flops, size):
    return pl.CostEstimate(flops=flops, bytes_accessed=size, transcendentals=0)


def shards(
    rhs_interior,
    rhs_interface,
    inv_blocks,
    coupling,
    interface_map,
    slot_counts,
    column_order,
    schur_inverse,
):
    f32, bf16 = F32, BF16
    nb, n = inv_blocks.shape[:2]
    k = coupling.shape[2]
    cols = rhs_interior.shape[1]
    owners = lax.axis_size(ALL)
    devs = lax.axis_size(DEV)
    secs = lax.axis_size(SEC)
    pairs = owners // 2
    slots = nb * k
    per_pair = slots // pairs
    half = per_pair // 2
    piece = rhs_interface.shape[0]
    pair_rows = 2 * piece
    band = piece * secs
    steps = nb // GROUP
    lanes = GROUP * k

    block_specs = [
        pl.BlockSpec((GROUP * n, cols), lambda i: (i, 0)),
        pl.BlockSpec((GROUP, n, n), lambda i: (i, 0, 0)),
    ]
    sent, place = pl.pallas_call(
        functools.partial(forward_kernel, (per_pair, half, pair_rows, pairs, devs)),
        grid_spec=pltpu.PrefetchScalarGridSpec(
            num_scalar_prefetch=1,
            grid=(steps,),
            in_specs=[
                pl.BlockSpec((nb, k), lambda i, at: (0, 0)),
                pl.BlockSpec((GROUP * n, cols), lambda i, at: (i, 0)),
                pl.BlockSpec((GROUP, n, n), lambda i, at: (i, 0, 0)),
                pl.BlockSpec((GROUP, None, k, n), lambda i, at: (i, 0, 0, 0)),
            ],
            out_specs=[
                pl.BlockSpec((owners * WIRE, cols), lambda i, at: (0, 0)),
                pl.BlockSpec((1, 1, lanes), lambda i, at: (i, 0, 0)),
            ],
            scratch_shapes=[
                pltpu.VMEM((2 * (owners * WIRE + 8), 128), f32),
                pltpu.VMEM((2 * lanes, 128), f32),
                pltpu.VMEM((pairs, 128), f32),
                pltpu.VMEM((pairs, 256), f32),
                pltpu.VMEM((2, 1, lanes), jnp.int32),
                pltpu.SMEM((2, 1, lanes), jnp.int32),
                pltpu.SemaphoreType.DMA((2,)),
            ],
        ),
        out_shape=[
            jax.ShapeDtypeStruct((owners * WIRE, cols), bf16),
            jax.ShapeDtypeStruct((steps, 1, lanes), jnp.int32),
        ],
        cost_estimate=cost(2 * 10**9, 14 * 10**6),
        name="forward",
    )(slot_counts, interface_map, rhs_interior, inv_blocks, coupling)
    got = exchange(sent.reshape(owners, WIRE, cols), ALL)
    solved, weights = pl.pallas_call(
        middle_kernel,
        grid=(steps,),
        in_specs=[*block_specs, pl.BlockSpec((GROUP, None, k, n), lambda i: (i, 1, 0, 0))],
        out_specs=[
            pl.BlockSpec((GROUP * n, cols), lambda i: (i, 0)),
            pl.BlockSpec((GROUP // 2, n, 2 * k), lambda i: (i, 0, 0)),
        ],
        out_shape=[
            jax.ShapeDtypeStruct((nb * n, cols), bf16),
            jax.ShapeDtypeStruct((nb // 2, n, 2 * k), bf16),
        ],
        cost_estimate=cost(2 * 10**9, 20 * 10**6),
        name="middle",
    )(rhs_interior, inv_blocks, coupling)

    core = lax.axis_index("c")
    offs = jnp.where(core == 0, got[:, half, :half], got[:, half, half : 2 * half])
    offs, solved, weights = lax.optimization_barrier((offs, solved, weights))
    target = jnp.pad(offs, ((0, 0), (0, WIRE - half)), constant_values=-1.0).reshape(1, -1)
    selector = jnp.arange(pair_rows, dtype=jnp.int32)[:, None].astype(bf16) == target
    arrived = jnp.dot(
        selector.astype(bf16), got.reshape(-1, cols), preferred_element_type=f32
    ).reshape(2, piece, cols)
    rhs_cols = jnp.take(rhs_interface, column_order, axis=1)
    mine = jnp.arange(2)[:, None, None] == core
    own = jnp.where(mine, rhs_cols[None], 0.0) - arrived
    reduced = own + lax.ppermute(own, "c", [(0, 1), (1, 0)])
    reduced = reduced.reshape(pair_rows, cols).astype(bf16)
    section = copies(reduced, "z").reshape(-1, cols)

    product = jnp.dot(schur_inverse, section, preferred_element_type=f32)
    parts = exchange(product.astype(bf16).reshape(secs, piece, cols), SEC)
    summed = jnp.sum(parts.astype(f32), axis=0).astype(bf16)
    values = copies(summed, SEC).reshape(band, cols)

    s = lax.axis_index(SEC)
    asked = lax.dynamic_slice_in_dim(got[:, half + 1 : half + 3], s * devs, devs, axis=0)
    asked = asked.reshape(devs, band // pair_rows, 64)[:, :, :per_pair]
    picker = asked[:, :, :, None] == jnp.arange(pair_rows, dtype=jnp.int32).astype(bf16)
    returned = jnp.einsum(
        "vjkr,jrn->vjkn",
        picker.astype(bf16),
        values.reshape(-1, pair_rows, cols),
        preferred_element_type=f32,
    ).astype(bf16)
    back = exchange(returned.reshape(devs, -1, cols), DEV).reshape(slots, cols)

    interior = pl.pallas_call(
        tail_kernel,
        grid_spec=pltpu.PrefetchScalarGridSpec(
            num_scalar_prefetch=1,
            grid=(steps,),
            in_specs=[
                pl.BlockSpec((slots, cols), lambda i, at: (0, 0)),
                pl.BlockSpec((GROUP * n, cols), lambda i, at: (i, 0)),
                pl.BlockSpec((GROUP // 2, n, 2 * k), lambda i, at: (i, 0, 0)),
            ],
            out_specs=pl.BlockSpec((GROUP * n, cols), lambda i, at: (i, 0)),
            scratch_shapes=[
                pltpu.VMEM((2 * (slots + 8), 128), f32),
                pltpu.VMEM((2 * lanes, 128), f32),
            ],
        ),
        out_shape=jax.ShapeDtypeStruct((nb * n, cols), bf16),
        cost_estimate=cost(4 * 10**9, 14 * 10**6),
        name="tail",
    )(jnp.pad(place.reshape(-1), (0, lanes), constant_values=2 * slots), back, solved, weights)
    return interior, values.astype(f32)


def solution(mesh):
    fine = Mesh(mesh.devices.reshape(4, 4, 4, 2), ALL)
    placed = (
        P(ALL, None),
        P(ALL, None),
        P(ALL, None, None),
        P(ALL, None, None, None),
        P(ALL, None),
        P(ALL),
        P(),
        P(DEV, SEC),
    )
    return jax.shard_map(
        shards,
        mesh=fine,
        in_specs=placed,
        out_specs=(P(ALL, None), P(DEV, None)),
        check_vma=False,
    )
```

```python
import functools

import jax
import jax.numpy as jnp
from jax import lax
from jax.experimental import pallas as pl
from jax.experimental.pallas import tpu as pltpu
from jax.sharding import Mesh
from jax.sharding import PartitionSpec as P

ALL = ("y", "x", "z", "c")
SEC = ("y", "x")
DEV = ("z", "c")
WIRE = 24
GROUP = 4
CHUNKS = 2
F32, BF16 = jnp.float32, jnp.bfloat16


def exchange(blocks, axis):
    return lax.all_to_all(blocks, axis, 0, 0, tiled=True)


def copies(array, axis):
    size = lax.axis_size(axis)
    return exchange(jnp.broadcast_to(array[None], (size, *array.shape)), axis)


def iota(shape, dim):
    return lax.broadcasted_iota(jnp.int32, shape, dim).astype(F32)


def quotient(x, n):
    return jnp.floor((x + 0.5) * (1.0 / n))


def dot(a, b, dims=((1,), (0,))):
    return lax.dot_general(a, b, (dims, ((), ())), preferred_element_type=F32)


def onehot(mask):
    return jnp.where(mask, 1.0, 0.0).astype(BF16)


def forward_kernel(
    sizes, counts_ref, map_ref, rhs_ref, inv_ref, couple_ref, out_ref, place_ref,
    wide_ref, stage_ref, base_ref, offs_ref, wire_ref, at_ref, sem
):
    per_pair, half, pair_rows, pairs, devs = sizes
    step = pl.program_id(0)
    n = inv_ref.shape[1]
    k = couple_ref.shape[1]
    lanes = GROUP * k
    rows_out = out_ref.shape[0]

    def handover(slot):
        return pltpu.make_async_copy(wire_ref.at[slot], at_ref.at[slot], sem.at[slot])

    @pl.when(step == 0)
    def _():
        stage_ref[...] = jnp.zeros_like(stage_ref)
        base_ref[...] = jnp.zeros_like(base_ref)
        offs_ref[...] = jnp.zeros_like(offs_ref)
        wire_ref[1] = jnp.full((1, lanes), 2 * rows_out, jnp.int32)

    def move(slot, first, last):
        for i in range(first, last):
            row = pl.ds(pl.multiple_of(at_ref[slot, 0, i], 2), 2)
            wide_ref[row, :] = stage_ref[2 * i : 2 * i + 2, :]

    for now in range(CHUNKS):
        before, c0 = 1 - now, now * GROUP
        first = step * (CHUNKS * GROUP) + c0
        slot = jnp.concatenate(
            [map_ref[pl.ds(first + b, 1), :] for b in range(GROUP)], axis=1
        ).astype(F32)
        at = lax.broadcasted_iota(jnp.int32, (1, k), 1)
        live = jnp.concatenate(
            [jnp.where(at < counts_ref[first + b], 1.0, 0.0) for b in range(GROUP)], axis=1
        )
        pair = quotient(slot, pair_rows)
        off = slot - pair_rows * pair
        table = jnp.where(iota((pairs, lanes), 0) == pair, 1.0, 0.0)
        earlier = dot(
            table.astype(BF16), onehot(iota((lanes, lanes), 0) < iota((lanes, lanes), 1))
        )
        rank = jnp.sum(table * (earlier + base_ref[:, :1]), axis=0, keepdims=True)
        base_ref[...] += jnp.sum(table, axis=1, keepdims=True)
        place = pair * per_pair + rank
        place_ref[now] = (2.0 * jnp.where(live == 0.0, pairs * per_pair, place)).astype(jnp.int32)
        wire = place + (WIRE - half) * quotient(place, half)
        wire_ref[now] = (2.0 * wire).astype(jnp.int32)
        row64 = (lax.broadcasted_iota(jnp.int32, (256, lanes), 0) & 63).astype(F32)
        offs_ref[...] += dot((table * off).astype(BF16), onehot(row64 == rank), ((1,), (1,)))

        if now == 0:

            @pl.when(step == 0)
            def _():
                handover(1).start()

        solved = [
            dot(inv_ref[b], rhs_ref[b * n : (b + 1) * n, :]).astype(BF16)
            for b in range(c0, c0 + GROUP)
        ]
        handover(before).wait()
        handover(now).start()
        move(before, 0, lanes // 2)
        parts = [dot(couple_ref[c0 + b], solved[b]) for b in range(GROUP)]
        move(before, lanes // 2, lanes)
        depth = lax.broadcasted_iota(jnp.int32, (k, 2 * 128), 0)
        for b in range(GROUP):
            part = jnp.where(depth < counts_ref[first + b], parts[b], 0.0)
            stage_ref[pl.ds(2 * b * k, k, stride=2), :] = part[:, :128]
            stage_ref[pl.ds(2 * b * k + 1, k, stride=2), :] = part[:, 128:]

    @pl.when(step == pl.num_programs(0) - 1)
    def _():
        handover(1).wait()
        move(1, 0, lanes)
        offs = offs_ref[...]
        p = lax.broadcasted_iota(jnp.int32, offs.shape, 0)
        lane = lax.broadcasted_iota(jnp.int32, offs.shape, 1)
        spread = jnp.where((lane >> 6) == (p & 3), offs, 0.0).astype(BF16)
        groups = pairs // 4
        member = iota((groups, pairs), 0) == quotient(iota((groups, pairs), 1), 4)
        wanted = dot(onehot(member), spread)
        level = lax.broadcasted_iota(jnp.int32, (2 * (WIRE - half), 128), 0)

        def spread_rows(parts, rest):
            for at, part in parts:
                rest = jnp.where(level == at, jnp.broadcast_to(part, level.shape), rest)
            return rest

        for v in range(devs):
            rows = [wanted[2 * v + r : 2 * v + r + 1, :] for r in range(2)]
            fixed = spread_rows(
                [(2 + 2 * r + h, rows[r][:, 128 * h : 128 * (h + 1)]) for r in range(2) for h in range(2)],
                jnp.zeros(level.shape, F32),
            )
            for d in range(v, rows_out // WIRE, devs):
                own = [(h, offs_ref[d // 2 : d // 2 + 1, 128 * h : 128 * (h + 1)]) for h in range(2)]
                w = 2 * (d * WIRE + half)
                wide_ref[w : w + 2 * (WIRE - half), :] = spread_rows(own, fixed)
        for t in range(rows_out // 256):
            rows = slice(256 * t, 256 * (t + 1))
            for h in range(2):
                out_ref[rows, 128 * h : 128 * (h + 1)] = wide_ref[
                    pl.ds(512 * t + h, 256, stride=2), :
                ].astype(BF16)


def middle_kernel(rhs_ref, inv_ref, couple_ref, solved_ref, w_ref):
    n = inv_ref.shape[1]
    for b in range(GROUP):
        rows = slice(b * n, (b + 1) * n)
        solved_ref[rows, :] = dot(inv_ref[b], rhs_ref[rows, :]).astype(BF16)
    for b in range(0, GROUP, 2):
        w_ref[b // 2] = jnp.concatenate(
            [dot(inv_ref[c], couple_ref[c], ((1,), (1,))) for c in (b, b + 1)], axis=1
        ).astype(BF16)


def tail_kernel(place_ref, back_ref, solved_ref, w_ref, out_ref, wide_ref, pick_ref):
    n = w_ref.shape[1]
    k = w_ref.shape[2] // 2
    group = 2 * w_ref.shape[0]
    slots = back_ref.shape[0]
    lanes = group * k
    step = pl.program_id(0)

    def gather(step, first, last):
        here = place_ref.at[pl.ds(step * lanes, lanes)]
        for i in range(first, last):
            row = pl.ds(pl.multiple_of(here[i], 2), 2)
            pick_ref[2 * i : 2 * i + 2, :] = wide_ref[row, :]

    @pl.when(step == 0)
    def _():
        for t in range(slots // 256):
            rows = slice(256 * t, 256 * (t + 1))
            for h in range(2):
                wide_ref[pl.ds(512 * t + h, 256, stride=2), :] = back_ref[
                    rows, 128 * h : 128 * (h + 1)
                ].astype(F32)
        wide_ref[2 * slots :, :] = jnp.zeros_like(wide_ref[2 * slots :, :])
        gather(step, 0, lanes)

    picked = jnp.concatenate(
        [pick_ref[pl.ds(h, lanes, stride=2), :] for h in range(2)], axis=1
    ).astype(BF16)
    empty = jnp.zeros((k, picked.shape[1]), BF16)
    for b in range(group):
        rows = slice(b * n, (b + 1) * n)
        own = picked[b * k : (b + 1) * k, :]
        pad = [own, empty] if b % 2 == 0 else [empty, own]
        term = dot(w_ref[b // 2], jnp.concatenate(pad, axis=0))
        gather(step + 1, b * k, (b + 1) * k)
        out_ref[rows, :] = (solved_ref[rows, :].astype(F32) - term).astype(BF16)


def cost(flops, size):
    return pl.CostEstimate(flops=flops, bytes_accessed=size, transcendentals=0)


def shards(
    rhs_interior,
    rhs_interface,
    inv_blocks,
    coupling,
    interface_map,
    slot_counts,
    column_order,
    schur_inverse,
):
    f32, bf16 = F32, BF16
    nb, n = inv_blocks.shape[:2]
    k = coupling.shape[2]
    cols = rhs_interior.shape[1]
    owners = lax.axis_size(ALL)
    devs = lax.axis_size(DEV)
    secs = lax.axis_size(SEC)
    pairs = owners // 2
    slots = nb * k
    per_pair = slots // pairs
    half = per_pair // 2
    piece = rhs_interface.shape[0]
    pair_rows = 2 * piece
    band = piece * secs
    steps = nb // GROUP
    lanes = GROUP * k

    block_specs = [
        pl.BlockSpec((GROUP * n, cols), lambda i: (i, 0)),
        pl.BlockSpec((GROUP, n, n), lambda i: (i, 0, 0)),
    ]
    wide = CHUNKS * GROUP
    sent, place = pl.pallas_call(
        functools.partial(forward_kernel, (per_pair, half, pair_rows, pairs, devs)),
        grid_spec=pltpu.PrefetchScalarGridSpec(
            num_scalar_prefetch=1,
            grid=(steps // CHUNKS,),
            in_specs=[
                pl.BlockSpec((nb, k), lambda i, at: (0, 0)),
                pl.BlockSpec((wide * n, cols), lambda i, at: (i, 0)),
                pl.BlockSpec((wide, n, n), lambda i, at: (i, 0, 0)),
                pl.BlockSpec((wide, None, k, n), lambda i, at: (i, 0, 0, 0)),
            ],
            out_specs=[
                pl.BlockSpec((owners * WIRE, cols), lambda i, at: (0, 0)),
                pl.BlockSpec((CHUNKS, 1, lanes), lambda i, at: (i, 0, 0)),
            ],
            scratch_shapes=[
                pltpu.VMEM((2 * (owners * WIRE + 8), 128), f32),
                pltpu.VMEM((2 * lanes, 128), f32),
                pltpu.VMEM((pairs, 128), f32),
                pltpu.VMEM((pairs, 256), f32),
                pltpu.VMEM((2, 1, lanes), jnp.int32),
                pltpu.SMEM((2, 1, lanes), jnp.int32),
                pltpu.SemaphoreType.DMA((2,)),
            ],
        ),
        out_shape=[
            jax.ShapeDtypeStruct((owners * WIRE, cols), bf16),
            jax.ShapeDtypeStruct((steps, 1, lanes), jnp.int32),
        ],
        cost_estimate=cost(2 * 10**9, 14 * 10**6),
        name="forward",
    )(slot_counts, interface_map, rhs_interior, inv_blocks, coupling)
    got = exchange(sent.reshape(owners, WIRE, cols), ALL)
    solved, weights = pl.pallas_call(
        middle_kernel,
        grid=(steps,),
        in_specs=[*block_specs, pl.BlockSpec((GROUP, None, k, n), lambda i: (i, 1, 0, 0))],
        out_specs=[
            pl.BlockSpec((GROUP * n, cols), lambda i: (i, 0)),
            pl.BlockSpec((GROUP // 2, n, 2 * k), lambda i: (i, 0, 0)),
        ],
        out_shape=[
            jax.ShapeDtypeStruct((nb * n, cols), bf16),
            jax.ShapeDtypeStruct((nb // 2, n, 2 * k), bf16),
        ],
        cost_estimate=cost(2 * 10**9, 20 * 10**6),
        name="middle",
    )(rhs_interior, inv_blocks, coupling)

    core = lax.axis_index("c")
    offs = jnp.where(core == 0, got[:, half, :half], got[:, half, half : 2 * half])
    offs, solved, weights = lax.optimization_barrier((offs, solved, weights))
    target = jnp.pad(offs, ((0, 0), (0, WIRE - half)), constant_values=-1.0).reshape(1, -1)
    selector = jnp.arange(pair_rows, dtype=jnp.int32)[:, None].astype(bf16) == target
    arrived = jnp.dot(
        selector.astype(bf16), got.reshape(-1, cols), preferred_element_type=f32
    ).reshape(2, piece, cols)
    rhs_cols = jnp.take(rhs_interface, column_order, axis=1)
    mine = jnp.arange(2)[:, None, None] == core
    own = jnp.where(mine, rhs_cols[None], 0.0) - arrived
    reduced = own + lax.ppermute(own, "c", [(0, 1), (1, 0)])
    reduced = reduced.reshape(pair_rows, cols).astype(bf16)
    section = copies(reduced, "z").reshape(-1, cols)

    product = jnp.dot(schur_inverse, section, preferred_element_type=f32)
    parts = exchange(product.astype(bf16).reshape(secs, piece, cols), SEC)
    summed = jnp.sum(parts.astype(f32), axis=0).astype(bf16)
    values = copies(summed, SEC).reshape(band, cols)

    s = lax.axis_index(SEC)
    asked = lax.dynamic_slice_in_dim(got[:, half + 1 : half + 3], s * devs, devs, axis=0)
    asked = asked.reshape(devs, band // pair_rows, 64)[:, :, :per_pair]
    picker = asked[:, :, :, None] == jnp.arange(pair_rows, dtype=jnp.int32).astype(bf16)
    returned = jnp.einsum(
        "vjkr,jrn->vjkn",
        picker.astype(bf16),
        values.reshape(-1, pair_rows, cols),
        preferred_element_type=f32,
    ).astype(bf16)
    back = exchange(returned.reshape(devs, -1, cols), DEV).reshape(slots, cols)

    interior = pl.pallas_call(
        tail_kernel,
        grid_spec=pltpu.PrefetchScalarGridSpec(
            num_scalar_prefetch=1,
            grid=(steps // CHUNKS,),
            in_specs=[
                pl.BlockSpec((slots, cols), lambda i, at: (0, 0)),
                pl.BlockSpec((wide * n, cols), lambda i, at: (i, 0)),
                pl.BlockSpec((wide // 2, n, 2 * k), lambda i, at: (i, 0, 0)),
            ],
            out_specs=pl.BlockSpec((wide * n, cols), lambda i, at: (i, 0)),
            scratch_shapes=[
                pltpu.VMEM((2 * (slots + 8), 128), f32),
                pltpu.VMEM((2 * wide * k, 128), f32),
            ],
        ),
        out_shape=jax.ShapeDtypeStruct((nb * n, cols), bf16),
        cost_estimate=cost(4 * 10**9, 14 * 10**6),
        name="tail",
    )(jnp.pad(place.reshape(-1), (0, wide * k), constant_values=2 * slots), back, solved, weights)
    return interior, values.astype(f32)


def solution(mesh):
    fine = Mesh(mesh.devices.reshape(4, 4, 4, 2), ALL)
    placed = (
        P(ALL, None),
        P(ALL, None),
        P(ALL, None, None),
        P(ALL, None, None, None),
        P(ALL, None),
        P(ALL),
        P(),
        P(DEV, SEC),
    )
    return jax.shard_map(
        shards,
        mesh=fine,
        in_specs=placed,
        out_specs=(P(ALL, None), P(DEV, None)),
        check_vma=False,
    )
```

```python
import functools

import jax
import jax.numpy as jnp
from jax import lax
from jax.experimental import pallas as pl
from jax.experimental.pallas import tpu as pltpu
from jax.sharding import Mesh
from jax.sharding import PartitionSpec as P

ALL = ("y", "x", "z", "c")
SEC = ("y", "x")
DEV = ("z", "c")
WIRE = 24
GROUP = 4
CHUNKS = 2
F32, BF16 = jnp.float32, jnp.bfloat16


def exchange(blocks, axis):
    return lax.all_to_all(blocks, axis, 0, 0, tiled=True)


def copies(array, axis):
    size = lax.axis_size(axis)
    return exchange(jnp.broadcast_to(array[None], (size, *array.shape)), axis)


def iota(shape, dim):
    return lax.broadcasted_iota(jnp.int32, shape, dim).astype(F32)


def quotient(x, n):
    return jnp.floor((x + 0.5) * (1.0 / n))


def dot(a, b, dims=((1,), (0,))):
    return lax.dot_general(a, b, (dims, ((), ())), preferred_element_type=F32)


def onehot(mask):
    return jnp.where(mask, 1.0, 0.0).astype(BF16)


def forward_kernel(
    sizes, counts_ref, map_ref, rhs_ref, inv_ref, couple_ref, out_ref, place_ref,
    wide_ref, stage_ref, base_ref, offs_ref, wire_ref, at_ref, sem
):
    per_pair, half, pair_rows, pairs, devs = sizes
    step = pl.program_id(0)
    n = inv_ref.shape[1]
    k = couple_ref.shape[1]
    lanes = GROUP * k
    rows_out = out_ref.shape[0]

    def handover(slot):
        return pltpu.make_async_copy(wire_ref.at[slot], at_ref.at[slot], sem.at[slot])

    @pl.when(step == 0)
    def _():
        stage_ref[...] = jnp.zeros_like(stage_ref)
        base_ref[...] = jnp.zeros_like(base_ref)
        offs_ref[...] = jnp.zeros_like(offs_ref)
        wire_ref[1] = jnp.full((1, lanes), 2 * rows_out, jnp.int32)

    def move(slot, first, last):
        for i in range(first, last):
            row = pl.ds(pl.multiple_of(at_ref[slot, 0, i], 2), 2)
            wide_ref[row, :] = stage_ref[2 * i : 2 * i + 2, :]

    for now in range(CHUNKS):
        before, c0 = 1 - now, now * GROUP
        first = step * (CHUNKS * GROUP) + c0
        slot = jnp.concatenate(
            [map_ref[pl.ds(first + b, 1), :] for b in range(GROUP)], axis=1
        ).astype(F32)
        at = lax.broadcasted_iota(jnp.int32, (1, k), 1)
        live = jnp.concatenate(
            [jnp.where(at < counts_ref[first + b], 1.0, 0.0) for b in range(GROUP)], axis=1
        )
        pair = quotient(slot, pair_rows)
        off = slot - pair_rows * pair
        table = jnp.where(iota((pairs, lanes), 0) == pair, 1.0, 0.0)
        earlier = dot(
            table.astype(BF16), onehot(iota((lanes, lanes), 0) < iota((lanes, lanes), 1))
        )
        rank = jnp.sum(table * (earlier + base_ref[:, :1]), axis=0, keepdims=True)
        base_ref[...] += jnp.sum(table, axis=1, keepdims=True)
        place = pair * per_pair + rank
        place_ref[now] = (2.0 * jnp.where(live == 0.0, pairs * per_pair, place)).astype(jnp.int32)
        wire = place + (WIRE - half) * quotient(place, half)
        wire_ref[now] = (2.0 * wire).astype(jnp.int32)
        row64 = (lax.broadcasted_iota(jnp.int32, (256, lanes), 0) & 63).astype(F32)
        offs_ref[...] += dot((table * off).astype(BF16), onehot(row64 == rank), ((1,), (1,)))

        if now == 0:

            @pl.when(step == 0)
            def _():
                handover(1).start()

        folded = [
            dot(couple_ref[b], inv_ref[b]).astype(BF16) for b in range(c0, c0 + GROUP)
        ]
        handover(before).wait()
        handover(now).start()
        move(before, 0, lanes // 2)
        parts = [
            dot(folded[b], rhs_ref[(c0 + b) * n : (c0 + b + 1) * n, :]) for b in range(GROUP)
        ]
        move(before, lanes // 2, lanes)
        depth = lax.broadcasted_iota(jnp.int32, (k, 2 * 128), 0)
        for b in range(GROUP):
            part = jnp.where(depth < counts_ref[first + b], parts[b], 0.0)
            stage_ref[pl.ds(2 * b * k, k, stride=2), :] = part[:, :128]
            stage_ref[pl.ds(2 * b * k + 1, k, stride=2), :] = part[:, 128:]

    @pl.when(step == pl.num_programs(0) - 1)
    def _():
        handover(1).wait()
        move(1, 0, lanes)
        offs = offs_ref[...]
        p = lax.broadcasted_iota(jnp.int32, offs.shape, 0)
        lane = lax.broadcasted_iota(jnp.int32, offs.shape, 1)
        spread = jnp.where((lane >> 6) == (p & 3), offs, 0.0).astype(BF16)
        groups = pairs // 4
        member = iota((groups, pairs), 0) == quotient(iota((groups, pairs), 1), 4)
        wanted = dot(onehot(member), spread)
        level = lax.broadcasted_iota(jnp.int32, (2 * (WIRE - half), 128), 0)

        def spread_rows(parts, rest):
            for at, part in parts:
                rest = jnp.where(level == at, jnp.broadcast_to(part, level.shape), rest)
            return rest

        for v in range(devs):
            rows = [wanted[2 * v + r : 2 * v + r + 1, :] for r in range(2)]
            fixed = spread_rows(
                [(2 + 2 * r + h, rows[r][:, 128 * h : 128 * (h + 1)]) for r in range(2) for h in range(2)],
                jnp.zeros(level.shape, F32),
            )
            for d in range(v, rows_out // WIRE, devs):
                own = [(h, offs_ref[d // 2 : d // 2 + 1, 128 * h : 128 * (h + 1)]) for h in range(2)]
                w = 2 * (d * WIRE + half)
                wide_ref[w : w + 2 * (WIRE - half), :] = spread_rows(own, fixed)
        for t in range(rows_out // 256):
            rows = slice(256 * t, 256 * (t + 1))
            for h in range(2):
                out_ref[rows, 128 * h : 128 * (h + 1)] = wide_ref[
                    pl.ds(512 * t + h, 256, stride=2), :
                ].astype(BF16)


def middle_kernel(rhs_ref, inv_ref, couple_ref, solved_ref, w_ref):
    n = inv_ref.shape[1]
    for b in range(GROUP):
        rows = slice(b * n, (b + 1) * n)
        solved_ref[rows, :] = dot(inv_ref[b], rhs_ref[rows, :]).astype(BF16)
    for b in range(0, GROUP, 2):
        w_ref[b // 2] = jnp.concatenate(
            [dot(inv_ref[c], couple_ref[c], ((1,), (1,))) for c in (b, b + 1)], axis=1
        ).astype(BF16)


def tail_kernel(place_ref, back_ref, solved_ref, w_ref, out_ref, wide_ref, pick_ref):
    n = w_ref.shape[1]
    k = w_ref.shape[2] // 2
    group = 2 * w_ref.shape[0]
    slots = back_ref.shape[0]
    lanes = group * k
    step = pl.program_id(0)

    def gather(step, first, last):
        here = place_ref.at[pl.ds(step * lanes, lanes)]
        for i in range(first, last):
            row = pl.ds(pl.multiple_of(here[i], 2), 2)
            pick_ref[2 * i : 2 * i + 2, :] = wide_ref[row, :]

    @pl.when(step == 0)
    def _():
        for t in range(slots // 256):
            rows = slice(256 * t, 256 * (t + 1))
            for h in range(2):
                wide_ref[pl.ds(512 * t + h, 256, stride=2), :] = back_ref[
                    rows, 128 * h : 128 * (h + 1)
                ].astype(F32)
        wide_ref[2 * slots :, :] = jnp.zeros_like(wide_ref[2 * slots :, :])
        gather(step, 0, lanes)

    picked = jnp.concatenate(
        [pick_ref[pl.ds(h, lanes, stride=2), :] for h in range(2)], axis=1
    ).astype(BF16)
    empty = jnp.zeros((k, picked.shape[1]), BF16)
    for b in range(group):
        rows = slice(b * n, (b + 1) * n)
        own = picked[b * k : (b + 1) * k, :]
        pad = [own, empty] if b % 2 == 0 else [empty, own]
        term = dot(w_ref[b // 2], jnp.concatenate(pad, axis=0))
        gather(step + 1, b * k, (b + 1) * k)
        out_ref[rows, :] = (solved_ref[rows, :].astype(F32) - term).astype(BF16)


def serve_kernel(asked_ref, values_ref, returned_ref, out_ref):
    peers, rows = returned_ref.shape[:2]
    count = asked_ref.shape[0] // peers
    per_pair = rows // peers
    depth = values_ref.shape[0] // peers
    out_ref[...] = values_ref[...].astype(F32)
    for j in range(peers):
        picker = asked_ref[j * count : (j + 1) * count, :] == iota((count, depth), 1)
        chosen = dot(onehot(picker), values_ref[j * depth : (j + 1) * depth, :])
        for v in range(peers):
            part = chosen[v * per_pair : (v + 1) * per_pair, :]
            returned_ref[v, j * per_pair : (j + 1) * per_pair, :] = part.astype(BF16)


def cost(flops, size):
    return pl.CostEstimate(flops=flops, bytes_accessed=size, transcendentals=0)


def shards(
    rhs_interior,
    rhs_interface,
    inv_blocks,
    coupling,
    interface_map,
    slot_counts,
    column_order,
    schur_inverse,
):
    f32, bf16 = F32, BF16
    nb, n = inv_blocks.shape[:2]
    k = coupling.shape[2]
    cols = rhs_interior.shape[1]
    owners = lax.axis_size(ALL)
    devs = lax.axis_size(DEV)
    secs = lax.axis_size(SEC)
    pairs = owners // 2
    slots = nb * k
    per_pair = slots // pairs
    half = per_pair // 2
    piece = rhs_interface.shape[0]
    pair_rows = 2 * piece
    band = piece * secs
    steps = nb // GROUP
    lanes = GROUP * k

    block_specs = [
        pl.BlockSpec((GROUP * n, cols), lambda i: (i, 0)),
        pl.BlockSpec((GROUP, n, n), lambda i: (i, 0, 0)),
    ]
    wide = CHUNKS * GROUP
    sent, place = pl.pallas_call(
        functools.partial(forward_kernel, (per_pair, half, pair_rows, pairs, devs)),
        grid_spec=pltpu.PrefetchScalarGridSpec(
            num_scalar_prefetch=1,
            grid=(steps // CHUNKS,),
            in_specs=[
                pl.BlockSpec((nb, k), lambda i, at: (0, 0)),
                pl.BlockSpec((wide * n, cols), lambda i, at: (i, 0)),
                pl.BlockSpec((wide, n, n), lambda i, at: (i, 0, 0)),
                pl.BlockSpec((wide, None, k, n), lambda i, at: (i, 0, 0, 0)),
            ],
            out_specs=[
                pl.BlockSpec((owners * WIRE, cols), lambda i, at: (0, 0)),
                pl.BlockSpec((CHUNKS, 1, lanes), lambda i, at: (i, 0, 0)),
            ],
            scratch_shapes=[
                pltpu.VMEM((2 * (owners * WIRE + 8), 128), f32),
                pltpu.VMEM((2 * lanes, 128), f32),
                pltpu.VMEM((pairs, 128), f32),
                pltpu.VMEM((pairs, 256), f32),
                pltpu.VMEM((2, 1, lanes), jnp.int32),
                pltpu.SMEM((2, 1, lanes), jnp.int32),
                pltpu.SemaphoreType.DMA((2,)),
            ],
        ),
        out_shape=[
            jax.ShapeDtypeStruct((owners * WIRE, cols), bf16),
            jax.ShapeDtypeStruct((steps, 1, lanes), jnp.int32),
        ],
        cost_estimate=cost(2 * 10**9, 14 * 10**6),
        name="forward",
    )(slot_counts, interface_map, rhs_interior, inv_blocks, coupling)
    got = exchange(sent.reshape(owners, WIRE, cols), ALL)
    solved, weights = pl.pallas_call(
        middle_kernel,
        grid=(steps,),
        in_specs=[*block_specs, pl.BlockSpec((GROUP, None, k, n), lambda i: (i, 1, 0, 0))],
        out_specs=[
            pl.BlockSpec((GROUP * n, cols), lambda i: (i, 0)),
            pl.BlockSpec((GROUP // 2, n, 2 * k), lambda i: (i, 0, 0)),
        ],
        out_shape=[
            jax.ShapeDtypeStruct((nb * n, cols), bf16),
            jax.ShapeDtypeStruct((nb // 2, n, 2 * k), bf16),
        ],
        cost_estimate=cost(2 * 10**9, 20 * 10**6),
        name="middle",
    )(rhs_interior, inv_blocks, coupling)

    core = lax.axis_index("c")
    offs = jnp.where(core == 0, got[:, half, :half], got[:, half, half : 2 * half])
    place = jnp.pad(place.reshape(-1), (0, wide * k), constant_values=2 * slots)
    offs, solved, weights, place = lax.optimization_barrier((offs, solved, weights, place))
    target = jnp.pad(offs, ((0, 0), (0, WIRE - half)), constant_values=-1.0).reshape(1, -1)
    selector = jnp.arange(pair_rows, dtype=jnp.int32)[:, None].astype(bf16) == target
    arrived = jnp.dot(
        selector.astype(bf16), got.reshape(-1, cols), preferred_element_type=f32
    ).reshape(2, piece, cols)
    rhs_cols = jnp.take(rhs_interface, column_order, axis=1)
    mine = jnp.arange(2)[:, None, None] == core
    own = jnp.where(mine, rhs_cols[None], 0.0) - arrived
    reduced = own + lax.ppermute(own, "c", [(0, 1), (1, 0)])
    reduced = reduced.reshape(pair_rows, cols).astype(bf16)
    section = copies(reduced, "z").reshape(-1, cols)

    product = jnp.dot(schur_inverse, section, preferred_element_type=f32)
    parts = exchange(product.astype(bf16).reshape(secs, piece, cols), SEC)
    summed = jnp.sum(parts.astype(f32), axis=0).astype(bf16)
    values = copies(summed, SEC).reshape(band, cols)

    s = lax.axis_index(SEC)
    asked = lax.dynamic_slice_in_dim(got[:, half + 1 : half + 3], s * devs, devs, axis=0)
    asked = asked.reshape(devs, band // pair_rows, 64)[:, :, :per_pair]
    asked = jnp.swapaxes(asked, 0, 1).astype(f32).reshape(slots, 1)
    whole = pl.BlockSpec(memory_space=pltpu.VMEM)
    returned, answer = pl.pallas_call(
        serve_kernel,
        in_specs=[whole, whole],
        out_specs=[whole, whole],
        out_shape=[
            jax.ShapeDtypeStruct((devs, slots // devs, cols), bf16),
            jax.ShapeDtypeStruct((band, cols), f32),
        ],
        compiler_params=pltpu.CompilerParams(vmem_limit_bytes=16 << 20),
        cost_estimate=cost(2 * 10**8, 4 * 10**6),
        name="serve",
    )(asked, values)
    back = exchange(returned, DEV).reshape(slots, cols)

    interior = pl.pallas_call(
        tail_kernel,
        grid_spec=pltpu.PrefetchScalarGridSpec(
            num_scalar_prefetch=1,
            grid=(steps // CHUNKS,),
            in_specs=[
                pl.BlockSpec((slots, cols), lambda i, at: (0, 0)),
                pl.BlockSpec((wide * n, cols), lambda i, at: (i, 0)),
                pl.BlockSpec((wide // 2, n, 2 * k), lambda i, at: (i, 0, 0)),
            ],
            out_specs=pl.BlockSpec((wide * n, cols), lambda i, at: (i, 0)),
            scratch_shapes=[
                pltpu.VMEM((2 * (slots + 8), 128), f32),
                pltpu.VMEM((2 * wide * k, 128), f32),
            ],
        ),
        out_shape=jax.ShapeDtypeStruct((nb * n, cols), bf16),
        cost_estimate=cost(4 * 10**9, 14 * 10**6),
        name="tail",
    )(place, back, solved, weights)
    return interior, answer


def solution(mesh):
    fine = Mesh(mesh.devices.reshape(4, 4, 4, 2), ALL)
    placed = (
        P(ALL, None),
        P(ALL, None),
        P(ALL, None, None),
        P(ALL, None, None, None),
        P(ALL, None),
        P(ALL),
        P(),
        P(DEV, SEC),
    )
    return jax.shard_map(
        shards,
        mesh=fine,
        in_specs=placed,
        out_specs=(P(ALL, None), P(DEV, None)),
        check_vma=False,
    )
```

```python
import functools

import jax
import jax.numpy as jnp
from jax import lax
from jax.experimental import pallas as pl
from jax.experimental.pallas import tpu as pltpu
from jax.sharding import Mesh
from jax.sharding import PartitionSpec as P

ALL = ("y", "x", "z", "c")
SEC = ("y", "x")
DEV = ("z", "c")
WIRE = 24
GROUP = 4
CHUNKS = 2
F32, BF16 = jnp.float32, jnp.bfloat16


def exchange(blocks, axis):
    return lax.all_to_all(blocks, axis, 0, 0, tiled=True)


def copies(array, axis):
    size = lax.axis_size(axis)
    return exchange(jnp.broadcast_to(array[None], (size, *array.shape)), axis)


def shifted(array, axis, by):
    size = lax.axis_size(axis)
    return lax.ppermute(array, axis, [(i, (i + by) % size) for i in range(size)])


def iota(shape, dim):
    return lax.broadcasted_iota(jnp.int32, shape, dim).astype(F32)


def quotient(x, n):
    return jnp.floor((x + 0.5) * (1.0 / n))


def dot(a, b, dims=((1,), (0,))):
    return lax.dot_general(a, b, (dims, ((), ())), preferred_element_type=F32)


def onehot(mask):
    return jnp.where(mask, 1.0, 0.0).astype(BF16)


def forward_kernel(
    sizes, counts_ref, map_ref, rhs_ref, inv_ref, couple_ref, out_ref, place_ref,
    wide_ref, stage_ref, base_ref, offs_ref, wire_ref, at_ref, sem
):
    per_pair, half, pair_rows, pairs, devs = sizes
    step = pl.program_id(0)
    n = inv_ref.shape[1]
    k = couple_ref.shape[1]
    lanes = GROUP * k
    rows_out = out_ref.shape[0]

    def handover(slot):
        return pltpu.make_async_copy(wire_ref.at[slot], at_ref.at[slot], sem.at[slot])

    @pl.when(step == 0)
    def _():
        stage_ref[...] = jnp.zeros_like(stage_ref)
        base_ref[...] = jnp.zeros_like(base_ref)
        offs_ref[...] = jnp.zeros_like(offs_ref)
        wire_ref[1] = jnp.full((1, lanes), 2 * rows_out, jnp.int32)

    def move(slot, first, last):
        for i in range(first, last):
            row = pl.ds(pl.multiple_of(at_ref[slot, 0, i], 2), 2)
            wide_ref[row, :] = stage_ref[2 * i : 2 * i + 2, :]

    for now in range(CHUNKS):
        before, c0 = 1 - now, now * GROUP
        first = step * (CHUNKS * GROUP) + c0
        slot = jnp.concatenate(
            [map_ref[pl.ds(first + b, 1), :] for b in range(GROUP)], axis=1
        ).astype(F32)
        at = lax.broadcasted_iota(jnp.int32, (1, k), 1)
        live = jnp.concatenate(
            [jnp.where(at < counts_ref[first + b], 1.0, 0.0) for b in range(GROUP)], axis=1
        )
        pair = quotient(slot, pair_rows)
        off = slot - pair_rows * pair
        table = jnp.where(iota((pairs, lanes), 0) == pair, 1.0, 0.0)
        earlier = dot(
            table.astype(BF16), onehot(iota((lanes, lanes), 0) < iota((lanes, lanes), 1))
        )
        rank = jnp.sum(table * (earlier + base_ref[:, :1]), axis=0, keepdims=True)
        base_ref[...] += jnp.sum(table, axis=1, keepdims=True)
        place = pair * per_pair + rank
        place_ref[now] = (2.0 * jnp.where(live == 0.0, pairs * per_pair, place)).astype(jnp.int32)
        wire = place + (WIRE - half) * quotient(place, half)
        wire_ref[now] = (2.0 * wire).astype(jnp.int32)
        row64 = (lax.broadcasted_iota(jnp.int32, (256, lanes), 0) & 63).astype(F32)
        offs_ref[...] += dot((table * off).astype(BF16), onehot(row64 == rank), ((1,), (1,)))

        if now == 0:

            @pl.when(step == 0)
            def _():
                handover(1).start()

        solved = [
            dot(inv_ref[b], rhs_ref[b * n : (b + 1) * n, :]).astype(BF16)
            for b in range(c0, c0 + GROUP)
        ]
        handover(before).wait()
        handover(now).start()
        move(before, 0, lanes // 2)
        parts = [dot(couple_ref[c0 + b], solved[b]) for b in range(GROUP)]
        move(before, lanes // 2, lanes)
        depth = lax.broadcasted_iota(jnp.int32, (k, 2 * 128), 0)
        for b in range(GROUP):
            part = jnp.where(depth < counts_ref[first + b], parts[b], 0.0)
            stage_ref[pl.ds(2 * b * k, k, stride=2), :] = part[:, :128]
            stage_ref[pl.ds(2 * b * k + 1, k, stride=2), :] = part[:, 128:]

    @pl.when(step == pl.num_programs(0) - 1)
    def _():
        handover(1).wait()
        move(1, 0, lanes)
        offs = offs_ref[...]
        p = lax.broadcasted_iota(jnp.int32, offs.shape, 0)
        lane = lax.broadcasted_iota(jnp.int32, offs.shape, 1)
        spread = jnp.where((lane >> 6) == (p & 3), offs, 0.0).astype(BF16)
        groups = pairs // 4
        member = iota((groups, pairs), 0) == quotient(iota((groups, pairs), 1), 4)
        wanted = dot(onehot(member), spread)
        level = lax.broadcasted_iota(jnp.int32, (2 * (WIRE - half), 128), 0)

        def spread_rows(parts, rest):
            for at, part in parts:
                rest = jnp.where(level == at, jnp.broadcast_to(part, level.shape), rest)
            return rest

        for v in range(devs):
            rows = [wanted[2 * v + r : 2 * v + r + 1, :] for r in range(2)]
            fixed = spread_rows(
                [(2 + 2 * r + h, rows[r][:, 128 * h : 128 * (h + 1)]) for r in range(2) for h in range(2)],
                jnp.zeros(level.shape, F32),
            )
            for d in range(v, rows_out // WIRE, devs):
                own = [(h, offs_ref[d // 2 : d // 2 + 1, 128 * h : 128 * (h + 1)]) for h in range(2)]
                w = 2 * (d * WIRE + half)
                wide_ref[w : w + 2 * (WIRE - half), :] = spread_rows(own, fixed)
        for t in range(rows_out // 256):
            rows = slice(256 * t, 256 * (t + 1))
            for h in range(2):
                out_ref[rows, 128 * h : 128 * (h + 1)] = wide_ref[
                    pl.ds(512 * t + h, 256, stride=2), :
                ].astype(BF16)


def middle_kernel(rhs_ref, inv_ref, couple_ref, solved_ref, w_ref):
    n = inv_ref.shape[1]
    for b in range(GROUP):
        rows = slice(b * n, (b + 1) * n)
        solved_ref[rows, :] = dot(inv_ref[b], rhs_ref[rows, :]).astype(BF16)
    for b in range(0, GROUP, 2):
        w_ref[b // 2] = jnp.concatenate(
            [dot(inv_ref[c], couple_ref[c], ((1,), (1,))) for c in (b, b + 1)], axis=1
        ).astype(BF16)


def tail_kernel(place_ref, *refs):
    *back_refs, solved_ref, w_ref, out_ref, wide_ref, pick_ref = refs
    n = w_ref.shape[1]
    k = w_ref.shape[2] // 2
    group = 2 * w_ref.shape[0]
    share = back_refs[0].shape[0]
    slots = share * len(back_refs)
    lanes = group * k
    step = pl.program_id(0)

    def gather(step, first, last):
        here = place_ref.at[pl.ds(step * lanes, lanes)]
        for i in range(first, last):
            row = pl.ds(pl.multiple_of(here[i], 2), 2)
            pick_ref[2 * i : 2 * i + 2, :] = wide_ref[row, :]

    @pl.when(step == 0)
    def _():
        for t, back_ref in enumerate(back_refs):
            for h in range(2):
                wide_ref[pl.ds(2 * share * t + h, share, stride=2), :] = back_ref[
                    :, 128 * h : 128 * (h + 1)
                ].astype(F32)
        wide_ref[2 * slots :, :] = jnp.zeros_like(wide_ref[2 * slots :, :])
        gather(step, 0, lanes)

    picked = jnp.concatenate(
        [pick_ref[pl.ds(h, lanes, stride=2), :] for h in range(2)], axis=1
    ).astype(BF16)
    empty = jnp.zeros((k, picked.shape[1]), BF16)
    for b in range(group):
        rows = slice(b * n, (b + 1) * n)
        own = picked[b * k : (b + 1) * k, :]
        pad = [own, empty] if b % 2 == 0 else [empty, own]
        term = dot(w_ref[b // 2], jnp.concatenate(pad, axis=0))
        gather(step + 1, b * k, (b + 1) * k)
        out_ref[rows, :] = (solved_ref[rows, :].astype(F32) - term).astype(BF16)


def serve_kernel(asked_ref, values_ref, *returned_refs):
    peers = len(returned_refs)
    rows = returned_refs[0].shape[0]
    count = asked_ref.shape[0] // peers
    per_pair = rows // peers
    depth = values_ref.shape[0] // peers
    for j in range(peers):
        picker = asked_ref[j * count : (j + 1) * count, :] == iota((count, depth), 1)
        chosen = dot(onehot(picker), values_ref[j * depth : (j + 1) * depth, :])
        for v in range(peers):
            part = chosen[v * per_pair : (v + 1) * per_pair, :]
            returned_refs[v][j * per_pair : (j + 1) * per_pair, :] = part.astype(BF16)


def cost(flops, size):
    return pl.CostEstimate(flops=flops, bytes_accessed=size, transcendentals=0)


def shards(
    rhs_interior,
    rhs_interface,
    inv_blocks,
    coupling,
    interface_map,
    slot_counts,
    column_order,
    schur_inverse,
):
    f32, bf16 = F32, BF16
    nb, n = inv_blocks.shape[:2]
    k = coupling.shape[2]
    cols = rhs_interior.shape[1]
    owners = lax.axis_size(ALL)
    devs = lax.axis_size(DEV)
    secs = lax.axis_size(SEC)
    pairs = owners // 2
    slots = nb * k
    per_pair = slots // pairs
    half = per_pair // 2
    piece = rhs_interface.shape[0]
    pair_rows = 2 * piece
    band = piece * secs
    steps = nb // GROUP
    lanes = GROUP * k

    block_specs = [
        pl.BlockSpec((GROUP * n, cols), lambda i: (i, 0)),
        pl.BlockSpec((GROUP, n, n), lambda i: (i, 0, 0)),
    ]
    wide = CHUNKS * GROUP
    sent, place = pl.pallas_call(
        functools.partial(forward_kernel, (per_pair, half, pair_rows, pairs, devs)),
        grid_spec=pltpu.PrefetchScalarGridSpec(
            num_scalar_prefetch=1,
            grid=(steps // CHUNKS,),
            in_specs=[
                pl.BlockSpec((nb, k), lambda i, at: (0, 0)),
                pl.BlockSpec((wide * n, cols), lambda i, at: (i, 0)),
                pl.BlockSpec((wide, n, n), lambda i, at: (i, 0, 0)),
                pl.BlockSpec((wide, None, k, n), lambda i, at: (i, 0, 0, 0)),
            ],
            out_specs=[
                pl.BlockSpec((owners * WIRE, cols), lambda i, at: (0, 0)),
                pl.BlockSpec((CHUNKS, 1, lanes), lambda i, at: (i, 0, 0)),
            ],
            scratch_shapes=[
                pltpu.VMEM((2 * (owners * WIRE + 8), 128), f32),
                pltpu.VMEM((2 * lanes, 128), f32),
                pltpu.VMEM((pairs, 128), f32),
                pltpu.VMEM((pairs, 256), f32),
                pltpu.VMEM((2, 1, lanes), jnp.int32),
                pltpu.SMEM((2, 1, lanes), jnp.int32),
                pltpu.SemaphoreType.DMA((2,)),
            ],
        ),
        out_shape=[
            jax.ShapeDtypeStruct((owners * WIRE, cols), bf16),
            jax.ShapeDtypeStruct((steps, 1, lanes), jnp.int32),
        ],
        cost_estimate=cost(2 * 10**9, 14 * 10**6),
        name="forward",
    )(slot_counts, interface_map, rhs_interior, inv_blocks, coupling)
    got = exchange(sent.reshape(owners, WIRE, cols), ALL)
    solved, weights = pl.pallas_call(
        middle_kernel,
        grid=(steps,),
        in_specs=[*block_specs, pl.BlockSpec((GROUP, None, k, n), lambda i: (i, 1, 0, 0))],
        out_specs=[
            pl.BlockSpec((GROUP * n, cols), lambda i: (i, 0)),
            pl.BlockSpec((GROUP // 2, n, 2 * k), lambda i: (i, 0, 0)),
        ],
        out_shape=[
            jax.ShapeDtypeStruct((nb * n, cols), bf16),
            jax.ShapeDtypeStruct((nb // 2, n, 2 * k), bf16),
        ],
        cost_estimate=cost(2 * 10**9, 20 * 10**6),
        name="middle",
    )(rhs_interior, inv_blocks, coupling)

    core = lax.axis_index("c")
    offs = jnp.where(core == 0, got[:, half, :half], got[:, half, half : 2 * half])
    me = lax.axis_index(DEV)
    share = 2 * slots // devs
    nearer = (me - place // share) % devs * share + place % share
    place = jnp.where(place < 2 * slots, nearer, place).reshape(-1)
    place = jnp.pad(place, (0, wide * k), constant_values=2 * slots)
    offs, solved, weights, place = lax.optimization_barrier((offs, solved, weights, place))
    target = jnp.pad(offs, ((0, 0), (0, WIRE - half)), constant_values=-1.0).reshape(1, -1)
    selector = jnp.arange(pair_rows, dtype=jnp.int32)[:, None].astype(bf16) == target
    arrived = jnp.dot(
        selector.astype(bf16), got.reshape(-1, cols), preferred_element_type=f32
    ).reshape(2, piece, cols)
    rhs_cols = jnp.take(rhs_interface, column_order, axis=1)
    mine = jnp.arange(2)[:, None, None] == core
    own = jnp.where(mine, rhs_cols[None], 0.0) - arrived
    reduced = own + lax.ppermute(own, "c", [(0, 1), (1, 0)])
    reduced = reduced.reshape(pair_rows, cols).astype(bf16)
    z = lax.axis_index("z")
    depth = lax.axis_size("z")
    near = [reduced] + [shifted(reduced, "z", by) for by in range(1, depth)]
    section = jnp.concatenate(
        [lax.select_n((z - at) % depth, *near) for at in range(depth)], axis=0
    )

    product = jnp.dot(schur_inverse, section, preferred_element_type=f32)
    parts = exchange(product.astype(bf16).reshape(secs, piece, cols), SEC)
    summed = jnp.sum(parts.astype(f32), axis=0).astype(bf16)
    values = copies(summed, SEC).reshape(band, cols)

    s = lax.axis_index(SEC)
    asked = lax.dynamic_slice_in_dim(got[:, half + 1 : half + 3], s * devs, devs, axis=0)
    asked = lax.dynamic_slice_in_dim(jnp.concatenate([asked, asked]), me, devs, axis=0)
    asked = asked.reshape(devs, band // pair_rows, 64)[:, :, :per_pair]
    asked = jnp.swapaxes(asked, 0, 1).astype(f32).reshape(slots, 1)
    whole = pl.BlockSpec(memory_space=pltpu.VMEM)
    pieces = pl.pallas_call(
        serve_kernel,
        in_specs=[whole, whole],
        out_specs=[whole] * devs,
        out_shape=[jax.ShapeDtypeStruct((slots // devs, cols), bf16)] * devs,
        compiler_params=pltpu.CompilerParams(vmem_limit_bytes=16 << 20),
        cost_estimate=cost(2 * 10**8, 4 * 10**6),
        name="serve",
    )(asked, values)
    back = [pieces[0]] + [shifted(pieces[by], DEV, by) for by in range(1, devs)]
    interior = pl.pallas_call(
        tail_kernel,
        grid_spec=pltpu.PrefetchScalarGridSpec(
            num_scalar_prefetch=1,
            grid=(steps // CHUNKS,),
            in_specs=[
                *[pl.BlockSpec((slots // devs, cols), lambda i, at: (0, 0))] * devs,
                pl.BlockSpec((wide * n, cols), lambda i, at: (i, 0)),
                pl.BlockSpec((wide // 2, n, 2 * k), lambda i, at: (i, 0, 0)),
            ],
            out_specs=pl.BlockSpec((wide * n, cols), lambda i, at: (i, 0)),
            scratch_shapes=[
                pltpu.VMEM((2 * (slots + 8), 128), f32),
                pltpu.VMEM((2 * wide * k, 128), f32),
            ],
        ),
        out_shape=jax.ShapeDtypeStruct((nb * n, cols), bf16),
        cost_estimate=cost(4 * 10**9, 14 * 10**6),
        name="tail",
    )(place, *back, solved, weights)
    return interior, values.astype(f32)


def solution(mesh):
    fine = Mesh(mesh.devices.reshape(4, 4, 4, 2), ALL)
    placed = (
        P(ALL, None),
        P(ALL, None),
        P(ALL, None, None),
        P(ALL, None, None, None),
        P(ALL, None),
        P(ALL),
        P(),
        P(DEV, SEC),
    )
    return jax.shard_map(
        shards,
        mesh=fine,
        in_specs=placed,
        out_specs=(P(ALL, None), P(DEV, None)),
        check_vma=False,
    )
```

```python
import functools

import jax
import jax.numpy as jnp
from jax import lax
from jax.experimental import pallas as pl
from jax.experimental.pallas import tpu as pltpu
from jax.sharding import Mesh
from jax.sharding import PartitionSpec as P

ALL = ("y", "x", "z", "c")
SEC = ("y", "x")
DEV = ("z", "c")
WIRE = 24
GROUP = 4
CHUNKS = 2
F32, BF16 = jnp.float32, jnp.bfloat16


def exchange(blocks, axis):
    return lax.all_to_all(blocks, axis, 0, 0, tiled=True)


def copies(array, axis):
    size = lax.axis_size(axis)
    return exchange(jnp.broadcast_to(array[None], (size, *array.shape)), axis)


def shifted(array, axis, by):
    size = lax.axis_size(axis)
    return lax.ppermute(array, axis, [(i, (i + by) % size) for i in range(size)])


def iota(shape, dim):
    return lax.broadcasted_iota(jnp.int32, shape, dim).astype(F32)


def quotient(x, n):
    return jnp.floor((x + 0.5) * (1.0 / n))


def dot(a, b, dims=((1,), (0,))):
    return lax.dot_general(a, b, (dims, ((), ())), preferred_element_type=F32)


def onehot(mask):
    return jnp.where(mask, 1.0, 0.0).astype(BF16)


def forward_kernel(
    sizes, counts_ref, map_ref, rhs_ref, inv_ref, couple_ref, out_ref, place_ref,
    wide_ref, stage_ref, base_ref, offs_ref, wire_ref, at_ref, sem
):
    per_pair, half, pair_rows, pairs, devs = sizes
    step = pl.program_id(0)
    n = inv_ref.shape[1]
    k = couple_ref.shape[1]
    lanes = GROUP * k
    rows_out = out_ref.shape[0]

    def handover(slot):
        return pltpu.make_async_copy(wire_ref.at[slot], at_ref.at[slot], sem.at[slot])

    @pl.when(step == 0)
    def _():
        stage_ref[...] = jnp.zeros_like(stage_ref)
        base_ref[...] = jnp.zeros_like(base_ref)
        offs_ref[...] = jnp.zeros_like(offs_ref)
        wire_ref[1] = jnp.full((1, lanes), 2 * rows_out, jnp.int32)

    def move(slot, first, last):
        for i in range(first, last):
            row = pl.ds(pl.multiple_of(at_ref[slot, 0, i], 2), 2)
            wide_ref[row, :] = stage_ref[2 * i : 2 * i + 2, :]

    for now in range(CHUNKS):
        before, c0 = 1 - now, now * GROUP
        first = step * (CHUNKS * GROUP) + c0
        slot = jnp.concatenate(
            [map_ref[pl.ds(first + b, 1), :] for b in range(GROUP)], axis=1
        ).astype(F32)
        at = lax.broadcasted_iota(jnp.int32, (1, k), 1)
        live = jnp.concatenate(
            [jnp.where(at < counts_ref[first + b], 1.0, 0.0) for b in range(GROUP)], axis=1
        )
        pair = quotient(slot, pair_rows)
        off = slot - pair_rows * pair
        table = jnp.where(iota((pairs, lanes), 0) == pair, 1.0, 0.0)
        earlier = dot(
            table.astype(BF16), onehot(iota((lanes, lanes), 0) < iota((lanes, lanes), 1))
        )
        rank = jnp.sum(table * (earlier + base_ref[:, :1]), axis=0, keepdims=True)
        base_ref[...] += jnp.sum(table, axis=1, keepdims=True)
        place = pair * per_pair + rank
        place_ref[now] = (2.0 * jnp.where(live == 0.0, pairs * per_pair, place)).astype(jnp.int32)
        wire = place + (WIRE - half) * quotient(place, half)
        wire_ref[now] = (2.0 * wire).astype(jnp.int32)
        row64 = (lax.broadcasted_iota(jnp.int32, (256, lanes), 0) & 63).astype(F32)
        offs_ref[...] += dot((table * off).astype(BF16), onehot(row64 == rank), ((1,), (1,)))

        if now == 0:

            @pl.when(step == 0)
            def _():
                handover(1).start()

        solved = [
            dot(inv_ref[b], rhs_ref[b * n : (b + 1) * n, :]).astype(BF16)
            for b in range(c0, c0 + GROUP)
        ]
        handover(before).wait()
        handover(now).start()
        move(before, 0, lanes // 2)
        parts = [dot(couple_ref[c0 + b], solved[b]) for b in range(GROUP)]
        move(before, lanes // 2, lanes)
        depth = lax.broadcasted_iota(jnp.int32, (k, 2 * 128), 0)
        for b in range(GROUP):
            part = jnp.where(depth < counts_ref[first + b], parts[b], 0.0)
            stage_ref[pl.ds(2 * b * k, k, stride=2), :] = part[:, :128]
            stage_ref[pl.ds(2 * b * k + 1, k, stride=2), :] = part[:, 128:]

    @pl.when(step == pl.num_programs(0) - 1)
    def _():
        handover(1).wait()
        move(1, 0, lanes)
        offs = offs_ref[...]
        p = lax.broadcasted_iota(jnp.int32, offs.shape, 0)
        lane = lax.broadcasted_iota(jnp.int32, offs.shape, 1)
        spread = jnp.where((lane >> 6) == (p & 3), offs, 0.0).astype(BF16)
        groups = pairs // 4
        member = iota((groups, pairs), 0) == quotient(iota((groups, pairs), 1), 4)
        wanted = dot(onehot(member), spread)
        level = lax.broadcasted_iota(jnp.int32, (2 * (WIRE - half), 128), 0)

        def spread_rows(parts, rest):
            for at, part in parts:
                rest = jnp.where(level == at, jnp.broadcast_to(part, level.shape), rest)
            return rest

        for v in range(devs):
            rows = [wanted[2 * v + r : 2 * v + r + 1, :] for r in range(2)]
            fixed = spread_rows(
                [(2 + 2 * r + h, rows[r][:, 128 * h : 128 * (h + 1)]) for r in range(2) for h in range(2)],
                jnp.zeros(level.shape, F32),
            )
            for d in range(v, rows_out // WIRE, devs):
                own = [(h, offs_ref[d // 2 : d // 2 + 1, 128 * h : 128 * (h + 1)]) for h in range(2)]
                w = 2 * (d * WIRE + half)
                wide_ref[w : w + 2 * (WIRE - half), :] = spread_rows(own, fixed)
        for t in range(rows_out // 256):
            rows = slice(256 * t, 256 * (t + 1))
            for h in range(2):
                out_ref[rows, 128 * h : 128 * (h + 1)] = wide_ref[
                    pl.ds(512 * t + h, 256, stride=2), :
                ].astype(BF16)


def middle_kernel(rhs_ref, inv_ref, couple_ref, solved_ref, w_ref):
    n = inv_ref.shape[1]
    for b in range(GROUP):
        rows = slice(b * n, (b + 1) * n)
        solved_ref[rows, :] = dot(inv_ref[b], rhs_ref[rows, :]).astype(BF16)
    for b in range(0, GROUP, 2):
        w_ref[b // 2] = jnp.concatenate(
            [dot(inv_ref[c], couple_ref[c], ((1,), (1,))) for c in (b, b + 1)], axis=1
        ).astype(BF16)


def tail_kernel(place_ref, *refs):
    *back_refs, solved_ref, w_ref, out_ref, wide_ref, pick_ref = refs
    n = w_ref.shape[1]
    k = w_ref.shape[2] // 2
    group = 2 * w_ref.shape[0]
    share = back_refs[0].shape[0]
    slots = share * len(back_refs)
    lanes = group * k
    step = pl.program_id(0)

    def gather(step, first, last):
        here = place_ref.at[pl.ds(step * lanes, lanes)]
        for i in range(first, last):
            row = pl.ds(pl.multiple_of(here[i], 2), 2)
            pick_ref[2 * i : 2 * i + 2, :] = wide_ref[row, :]

    @pl.when(step == 0)
    def _():
        for t, back_ref in enumerate(back_refs):
            for h in range(2):
                wide_ref[pl.ds(2 * share * t + h, share, stride=2), :] = back_ref[
                    :, 128 * h : 128 * (h + 1)
                ].astype(F32)
        wide_ref[2 * slots :, :] = jnp.zeros_like(wide_ref[2 * slots :, :])
        gather(step, 0, lanes)

    picked = jnp.concatenate(
        [pick_ref[pl.ds(h, lanes, stride=2), :] for h in range(2)], axis=1
    ).astype(BF16)
    empty = jnp.zeros((k, picked.shape[1]), BF16)
    for b in range(group):
        rows = slice(b * n, (b + 1) * n)
        own = picked[b * k : (b + 1) * k, :]
        pad = [own, empty] if b % 2 == 0 else [empty, own]
        term = dot(w_ref[b // 2], jnp.concatenate(pad, axis=0))
        gather(step + 1, b * k, (b + 1) * k)
        out_ref[rows, :] = (solved_ref[rows, :].astype(F32) - term).astype(BF16)


def serve_kernel(asked_ref, values_ref, *returned_refs):
    peers = len(returned_refs)
    rows = returned_refs[0].shape[0]
    count = asked_ref.shape[2]
    per_pair = rows // peers
    depth = values_ref.shape[0] // peers
    for j in range(peers):
        picker = onehot(asked_ref[j] == iota((depth, count), 0))
        chosen = dot(picker, values_ref[j * depth : (j + 1) * depth, :], ((0,), (0,)))
        for v in range(peers):
            part = chosen[v * per_pair : (v + 1) * per_pair, :]
            returned_refs[v][j * per_pair : (j + 1) * per_pair, :] = part.astype(BF16)


def cost(flops, size):
    return pl.CostEstimate(flops=flops, bytes_accessed=size, transcendentals=0)


def shards(
    rhs_interior,
    rhs_interface,
    inv_blocks,
    coupling,
    interface_map,
    slot_counts,
    column_order,
    schur_inverse,
):
    f32, bf16 = F32, BF16
    nb, n = inv_blocks.shape[:2]
    k = coupling.shape[2]
    cols = rhs_interior.shape[1]
    owners = lax.axis_size(ALL)
    devs = lax.axis_size(DEV)
    secs = lax.axis_size(SEC)
    pairs = owners // 2
    slots = nb * k
    per_pair = slots // pairs
    half = per_pair // 2
    piece = rhs_interface.shape[0]
    pair_rows = 2 * piece
    band = piece * secs
    steps = nb // GROUP
    lanes = GROUP * k

    block_specs = [
        pl.BlockSpec((GROUP * n, cols), lambda i: (i, 0)),
        pl.BlockSpec((GROUP, n, n), lambda i: (i, 0, 0)),
    ]
    wide = CHUNKS * GROUP
    sent, place = pl.pallas_call(
        functools.partial(forward_kernel, (per_pair, half, pair_rows, pairs, devs)),
        grid_spec=pltpu.PrefetchScalarGridSpec(
            num_scalar_prefetch=1,
            grid=(steps // CHUNKS,),
            in_specs=[
                pl.BlockSpec((nb, k), lambda i, at: (0, 0)),
                pl.BlockSpec((wide * n, cols), lambda i, at: (i, 0)),
                pl.BlockSpec((wide, n, n), lambda i, at: (i, 0, 0)),
                pl.BlockSpec((wide, None, k, n), lambda i, at: (i, 0, 0, 0)),
            ],
            out_specs=[
                pl.BlockSpec((owners * WIRE, cols), lambda i, at: (0, 0)),
                pl.BlockSpec((CHUNKS, 1, lanes), lambda i, at: (i, 0, 0)),
            ],
            scratch_shapes=[
                pltpu.VMEM((2 * (owners * WIRE + 8), 128), f32),
                pltpu.VMEM((2 * lanes, 128), f32),
                pltpu.VMEM((pairs, 128), f32),
                pltpu.VMEM((pairs, 256), f32),
                pltpu.VMEM((2, 1, lanes), jnp.int32),
                pltpu.SMEM((2, 1, lanes), jnp.int32),
                pltpu.SemaphoreType.DMA((2,)),
            ],
        ),
        out_shape=[
            jax.ShapeDtypeStruct((owners * WIRE, cols), bf16),
            jax.ShapeDtypeStruct((steps, 1, lanes), jnp.int32),
        ],
        cost_estimate=cost(2 * 10**9, 14 * 10**6),
        name="forward",
    )(slot_counts, interface_map, rhs_interior, inv_blocks, coupling)
    got = exchange(sent.reshape(owners, WIRE, cols), ALL)
    solved, weights = pl.pallas_call(
        middle_kernel,
        grid=(steps,),
        in_specs=[*block_specs, pl.BlockSpec((GROUP, None, k, n), lambda i: (i, 1, 0, 0))],
        out_specs=[
            pl.BlockSpec((GROUP * n, cols), lambda i: (i, 0)),
            pl.BlockSpec((GROUP // 2, n, 2 * k), lambda i: (i, 0, 0)),
        ],
        out_shape=[
            jax.ShapeDtypeStruct((nb * n, cols), bf16),
            jax.ShapeDtypeStruct((nb // 2, n, 2 * k), bf16),
        ],
        cost_estimate=cost(2 * 10**9, 20 * 10**6),
        name="middle",
    )(rhs_interior, inv_blocks, coupling)

    core = lax.axis_index("c")
    offs = jnp.where(core == 0, got[:, half, :half], got[:, half, half : 2 * half])
    me = lax.axis_index(DEV)
    share = 2 * slots // devs
    nearer = (me - place // share) % devs * share + place % share
    place = jnp.where(place < 2 * slots, nearer, place).reshape(-1)
    place = jnp.pad(place, (0, wide * k), constant_values=2 * slots)
    offs, solved, weights, place = lax.optimization_barrier((offs, solved, weights, place))
    target = jnp.pad(offs, ((0, 0), (0, WIRE - half)), constant_values=-1.0).reshape(1, -1)
    selector = jnp.arange(pair_rows, dtype=jnp.int32)[:, None].astype(bf16) == target
    arrived = jnp.dot(
        selector.astype(bf16), got.reshape(-1, cols), preferred_element_type=f32
    ).reshape(2, piece, cols)
    rhs_cols = jnp.take(rhs_interface, column_order, axis=1)
    mine = jnp.arange(2)[:, None, None] == core
    own = jnp.where(mine, rhs_cols[None], 0.0) - arrived
    reduced = own + lax.ppermute(own, "c", [(0, 1), (1, 0)])
    reduced = reduced.reshape(pair_rows, cols).astype(bf16)
    z = lax.axis_index("z")
    depth = lax.axis_size("z")
    near = [reduced] + [shifted(reduced, "z", by) for by in range(1, depth)]
    section = jnp.concatenate(
        [lax.select_n((z - at) % depth, *near) for at in range(depth)], axis=0
    )

    product = jnp.dot(schur_inverse, section, preferred_element_type=f32)
    parts = exchange(product.astype(bf16).reshape(secs, piece, cols), SEC)
    summed = jnp.sum(parts.astype(f32), axis=0).astype(bf16)
    values = copies(summed, SEC).reshape(band, cols)

    s = lax.axis_index(SEC)
    asked = lax.dynamic_slice_in_dim(got[:, half + 1 : half + 3], s * devs, devs, axis=0)
    asked = lax.dynamic_slice_in_dim(jnp.concatenate([asked, asked]), me, devs, axis=0)
    asked = asked.reshape(devs, band // pair_rows, 64)[:, :, :per_pair]
    asked = jnp.swapaxes(asked, 0, 1).astype(f32).reshape(devs, 1, slots // devs)
    whole = pl.BlockSpec(memory_space=pltpu.VMEM)
    pieces = pl.pallas_call(
        serve_kernel,
        in_specs=[whole, whole],
        out_specs=[whole] * devs,
        out_shape=[jax.ShapeDtypeStruct((slots // devs, cols), bf16)] * devs,
        compiler_params=pltpu.CompilerParams(vmem_limit_bytes=16 << 20),
        cost_estimate=cost(2 * 10**8, 4 * 10**6),
        name="serve",
    )(asked, values)
    back = [pieces[0]] + [shifted(pieces[by], DEV, by) for by in range(1, devs)]
    interior = pl.pallas_call(
        tail_kernel,
        grid_spec=pltpu.PrefetchScalarGridSpec(
            num_scalar_prefetch=1,
            grid=(steps // CHUNKS,),
            in_specs=[
                *[pl.BlockSpec((slots // devs, cols), lambda i, at: (0, 0))] * devs,
                pl.BlockSpec((wide * n, cols), lambda i, at: (i, 0)),
                pl.BlockSpec((wide // 2, n, 2 * k), lambda i, at: (i, 0, 0)),
            ],
            out_specs=pl.BlockSpec((wide * n, cols), lambda i, at: (i, 0)),
            scratch_shapes=[
                pltpu.VMEM((2 * (slots + 8), 128), f32),
                pltpu.VMEM((2 * wide * k, 128), f32),
            ],
        ),
        out_shape=jax.ShapeDtypeStruct((nb * n, cols), bf16),
        cost_estimate=cost(4 * 10**9, 14 * 10**6),
        compiler_params=pltpu.CompilerParams(vmem_limit_bytes=52 << 20),
        name="tail",
    )(place, *back, solved, weights)
    return interior, values.astype(f32)


def solution(mesh):
    fine = Mesh(mesh.devices.reshape(4, 4, 4, 2), ALL)
    placed = (
        P(ALL, None),
        P(ALL, None),
        P(ALL, None, None),
        P(ALL, None, None, None),
        P(ALL, None),
        P(ALL),
        P(),
        P(DEV, SEC),
    )
    return jax.shard_map(
        shards,
        mesh=fine,
        in_specs=placed,
        out_specs=(P(ALL, None), P(DEV, None)),
        check_vma=False,
    )
```

```python
import functools

import jax
import jax.numpy as jnp
from jax import lax
from jax.experimental import pallas as pl
from jax.experimental.pallas import tpu as pltpu
from jax.sharding import Mesh
from jax.sharding import PartitionSpec as P

ALL = ("y", "x", "z", "c")
SEC = ("y", "x")
DEV = ("z", "c")
WIRE = 24
GROUP = 4
CHUNKS = 2
F32, BF16 = jnp.float32, jnp.bfloat16


def exchange(blocks, axis):
    return lax.all_to_all(blocks, axis, 0, 0, tiled=True)


def copies(array, axis):
    size = lax.axis_size(axis)
    return exchange(jnp.broadcast_to(array[None], (size, *array.shape)), axis)


def shifted(array, axis, by):
    size = lax.axis_size(axis)
    return lax.ppermute(array, axis, [(i, (i + by) % size) for i in range(size)])


def iota(shape, dim):
    return lax.broadcasted_iota(jnp.int32, shape, dim).astype(F32)


def quotient(x, n):
    return jnp.floor((x + 0.5) * (1.0 / n))


def dot(a, b, dims=((1,), (0,))):
    return lax.dot_general(a, b, (dims, ((), ())), preferred_element_type=F32)


def onehot(mask):
    return jnp.where(mask, 1.0, 0.0).astype(BF16)


def forward_kernel(
    sizes, counts_ref, map_ref, rhs_ref, inv_ref, couple_ref, out_ref, place_ref,
    wide_ref, stage_ref, base_ref, offs_ref, wire_ref, at_ref, sem
):
    per_pair, half, pair_rows, pairs, devs = sizes
    step = pl.program_id(0)
    n = inv_ref.shape[1]
    k = couple_ref.shape[1]
    lanes = GROUP * k
    rows_out = out_ref.shape[0]

    def handover(slot):
        return pltpu.make_async_copy(wire_ref.at[slot], at_ref.at[slot], sem.at[slot])

    @pl.when(step == 0)
    def _():
        stage_ref[...] = jnp.zeros_like(stage_ref)
        base_ref[...] = jnp.zeros_like(base_ref)
        offs_ref[...] = jnp.zeros_like(offs_ref)
        wire_ref[1] = jnp.full((1, lanes), 2 * rows_out, jnp.int32)

    def move(slot, first, last):
        for i in range(first, last):
            row = pl.ds(pl.multiple_of(at_ref[slot, 0, i], 2), 2)
            wide_ref[row, :] = stage_ref[2 * i : 2 * i + 2, :]

    for now in range(CHUNKS):
        before, c0 = 1 - now, now * GROUP
        first = step * (CHUNKS * GROUP) + c0
        slot = jnp.concatenate(
            [map_ref[pl.ds(first + b, 1), :] for b in range(GROUP)], axis=1
        ).astype(F32)
        at = lax.broadcasted_iota(jnp.int32, (1, k), 1)
        live = jnp.concatenate(
            [jnp.where(at < counts_ref[first + b], 1.0, 0.0) for b in range(GROUP)], axis=1
        )
        pair = quotient(slot, pair_rows)
        off = slot - pair_rows * pair
        table = jnp.where(iota((pairs, lanes), 0) == pair, 1.0, 0.0)
        earlier = dot(
            table.astype(BF16), onehot(iota((lanes, lanes), 0) < iota((lanes, lanes), 1))
        )
        rank = jnp.sum(table * (earlier + base_ref[:, :1]), axis=0, keepdims=True)
        base_ref[...] += jnp.sum(table, axis=1, keepdims=True)
        place = pair * per_pair + rank
        place_ref[now] = (2.0 * jnp.where(live == 0.0, pairs * per_pair, place)).astype(jnp.int32)
        wire = place + (WIRE - half) * quotient(place, half)
        wire_ref[now] = (2.0 * wire).astype(jnp.int32)
        row64 = (lax.broadcasted_iota(jnp.int32, (256, lanes), 0) & 63).astype(F32)
        offs_ref[...] += dot((table * off).astype(BF16), onehot(row64 == rank), ((1,), (1,)))

        if now == 0:

            @pl.when(step == 0)
            def _():
                handover(1).start()

        solved = [
            dot(inv_ref[b], rhs_ref[b * n : (b + 1) * n, :]).astype(BF16)
            for b in range(c0, c0 + GROUP)
        ]
        handover(before).wait()
        handover(now).start()
        move(before, 0, lanes // 2)
        parts = [dot(couple_ref[c0 + b], solved[b]) for b in range(GROUP)]
        move(before, lanes // 2, lanes)
        depth = lax.broadcasted_iota(jnp.int32, (k, 2 * 128), 0)
        for b in range(GROUP):
            part = jnp.where(depth < counts_ref[first + b], parts[b], 0.0)
            stage_ref[pl.ds(2 * b * k, k, stride=2), :] = part[:, :128]
            stage_ref[pl.ds(2 * b * k + 1, k, stride=2), :] = part[:, 128:]

    @pl.when(step == pl.num_programs(0) - 1)
    def _():
        handover(1).wait()
        move(1, 0, lanes)
        offs = offs_ref[...]
        p = lax.broadcasted_iota(jnp.int32, offs.shape, 0)
        lane = lax.broadcasted_iota(jnp.int32, offs.shape, 1)
        spread = jnp.where((lane >> 6) == (p & 3), offs, 0.0).astype(BF16)
        groups = pairs // 4
        member = iota((groups, pairs), 0) == quotient(iota((groups, pairs), 1), 4)
        wanted = dot(onehot(member), spread)
        level = lax.broadcasted_iota(jnp.int32, (2 * (WIRE - half), 128), 0)

        def spread_rows(parts, rest):
            for at, part in parts:
                rest = jnp.where(level == at, jnp.broadcast_to(part, level.shape), rest)
            return rest

        for v in range(devs):
            rows = [wanted[2 * v + r : 2 * v + r + 1, :] for r in range(2)]
            fixed = spread_rows(
                [(2 + 2 * r + h, rows[r][:, 128 * h : 128 * (h + 1)]) for r in range(2) for h in range(2)],
                jnp.zeros(level.shape, F32),
            )
            for d in range(v, rows_out // WIRE, devs):
                own = [(h, offs_ref[d // 2 : d // 2 + 1, 128 * h : 128 * (h + 1)]) for h in range(2)]
                w = 2 * (d * WIRE + half)
                wide_ref[w : w + 2 * (WIRE - half), :] = spread_rows(own, fixed)
        for t in range(rows_out // 256):
            rows = slice(256 * t, 256 * (t + 1))
            for h in range(2):
                out_ref[rows, 128 * h : 128 * (h + 1)] = wide_ref[
                    pl.ds(512 * t + h, 256, stride=2), :
                ].astype(BF16)


def middle_kernel(rhs_ref, inv_ref, couple_ref, solved_ref, w_ref):
    n = inv_ref.shape[1]
    for b in range(GROUP):
        rows = slice(b * n, (b + 1) * n)
        solved_ref[rows, :] = dot(inv_ref[b], rhs_ref[rows, :]).astype(BF16)
    for b in range(0, GROUP, 2):
        w_ref[b // 2] = jnp.concatenate(
            [dot(inv_ref[c], couple_ref[c], ((1,), (1,))) for c in (b, b + 1)], axis=1
        ).astype(BF16)


def tail_kernel(place_ref, *refs):
    *back_refs, solved_ref, w_ref, out_ref, wide_ref, pick_ref = refs
    n = w_ref.shape[1]
    k = w_ref.shape[2] // 2
    group = 2 * w_ref.shape[0]
    share = back_refs[0].shape[0]
    slots = share * len(back_refs)
    lanes = group * k
    step = pl.program_id(0)

    def gather(step, first, last):
        here = place_ref.at[pl.ds(step * lanes, lanes)]
        for i in range(first, last):
            row = pl.ds(pl.multiple_of(here[i], 2), 2)
            pick_ref[2 * i : 2 * i + 2, :] = wide_ref[row, :]

    @pl.when(step == 0)
    def _():
        for t, back_ref in enumerate(back_refs):
            for h in range(2):
                wide_ref[pl.ds(2 * share * t + h, share, stride=2), :] = back_ref[
                    :, 128 * h : 128 * (h + 1)
                ].astype(F32)
        wide_ref[2 * slots :, :] = jnp.zeros_like(wide_ref[2 * slots :, :])
        gather(step, 0, lanes)

    picked = jnp.concatenate(
        [pick_ref[pl.ds(h, lanes, stride=2), :] for h in range(2)], axis=1
    ).astype(BF16)
    empty = jnp.zeros((k, picked.shape[1]), BF16)
    for b in range(group):
        rows = slice(b * n, (b + 1) * n)
        own = picked[b * k : (b + 1) * k, :]
        pad = [own, empty] if b % 2 == 0 else [empty, own]
        term = dot(w_ref[b // 2], jnp.concatenate(pad, axis=0))
        gather(step + 1, b * k, (b + 1) * k)
        out_ref[rows, :] = (solved_ref[rows, :].astype(F32) - term).astype(BF16)


def serve_kernel(asked_ref, values_ref, *returned_refs):
    peers = len(returned_refs)
    rows = returned_refs[0].shape[0]
    count = asked_ref.shape[2]
    per_pair = rows // peers
    depth = values_ref.shape[0] // peers
    for j in range(peers):
        picker = onehot(asked_ref[j] == iota((depth, count), 0))
        chosen = dot(picker, values_ref[j * depth : (j + 1) * depth, :], ((0,), (0,)))
        for v in range(peers):
            part = chosen[v * per_pair : (v + 1) * per_pair, :]
            returned_refs[v][j * per_pair : (j + 1) * per_pair, :] = part.astype(BF16)


def cost(flops, size):
    return pl.CostEstimate(flops=flops, bytes_accessed=size, transcendentals=0)


def shards(
    rhs_interior,
    rhs_interface,
    inv_blocks,
    coupling,
    interface_map,
    slot_counts,
    column_order,
    schur_inverse,
):
    f32, bf16 = F32, BF16
    nb, n = inv_blocks.shape[:2]
    k = coupling.shape[2]
    cols = rhs_interior.shape[1]
    owners = lax.axis_size(ALL)
    devs = lax.axis_size(DEV)
    secs = lax.axis_size(SEC)
    pairs = owners // 2
    slots = nb * k
    per_pair = slots // pairs
    half = per_pair // 2
    piece = rhs_interface.shape[0]
    pair_rows = 2 * piece
    band = piece * secs
    steps = nb // GROUP
    lanes = GROUP * k

    block_specs = [
        pl.BlockSpec((GROUP * n, cols), lambda i: (i, 0)),
        pl.BlockSpec((GROUP, n, n), lambda i: (i, 0, 0)),
    ]
    wide = CHUNKS * GROUP
    sent, place = pl.pallas_call(
        functools.partial(forward_kernel, (per_pair, half, pair_rows, pairs, devs)),
        grid_spec=pltpu.PrefetchScalarGridSpec(
            num_scalar_prefetch=1,
            grid=(steps // CHUNKS,),
            in_specs=[
                pl.BlockSpec((nb, k), lambda i, at: (0, 0)),
                pl.BlockSpec((wide * n, cols), lambda i, at: (i, 0)),
                pl.BlockSpec((wide, n, n), lambda i, at: (i, 0, 0)),
                pl.BlockSpec((wide, None, k, n), lambda i, at: (i, 0, 0, 0)),
            ],
            out_specs=[
                pl.BlockSpec((owners * WIRE, cols), lambda i, at: (0, 0)),
                pl.BlockSpec((CHUNKS, 1, lanes), lambda i, at: (i, 0, 0)),
            ],
            scratch_shapes=[
                pltpu.VMEM((2 * (owners * WIRE + 8), 128), f32),
                pltpu.VMEM((2 * lanes, 128), f32),
                pltpu.VMEM((pairs, 128), f32),
                pltpu.VMEM((pairs, 256), f32),
                pltpu.VMEM((2, 1, lanes), jnp.int32),
                pltpu.SMEM((2, 1, lanes), jnp.int32),
                pltpu.SemaphoreType.DMA((2,)),
            ],
        ),
        out_shape=[
            jax.ShapeDtypeStruct((owners * WIRE, cols), bf16),
            jax.ShapeDtypeStruct((steps, 1, lanes), jnp.int32),
        ],
        cost_estimate=cost(2 * 10**9, 14 * 10**6),
        name="forward",
    )(slot_counts, interface_map, rhs_interior, inv_blocks, coupling)
    got = exchange(sent.reshape(owners, WIRE, cols), ALL)
    solved, weights = pl.pallas_call(
        middle_kernel,
        grid=(steps,),
        in_specs=[*block_specs, pl.BlockSpec((GROUP, None, k, n), lambda i: (i, 1, 0, 0))],
        out_specs=[
            pl.BlockSpec((GROUP * n, cols), lambda i: (i, 0)),
            pl.BlockSpec((GROUP // 2, n, 2 * k), lambda i: (i, 0, 0)),
        ],
        out_shape=[
            jax.ShapeDtypeStruct((nb * n, cols), bf16),
            jax.ShapeDtypeStruct((nb // 2, n, 2 * k), bf16),
        ],
        cost_estimate=cost(2 * 10**9, 20 * 10**6),
        name="middle",
    )(rhs_interior, inv_blocks, coupling)

    core = lax.axis_index("c")
    offs = jnp.where(core == 0, got[:, half, :half], got[:, half, half : 2 * half])
    me = lax.axis_index(DEV)
    share = 2 * slots // devs
    nearer = (me - place // share) % devs * share + place % share
    place = jnp.where(place < 2 * slots, nearer, place).reshape(-1)
    place = jnp.pad(place, (0, wide * k), constant_values=2 * slots)
    offs, solved, weights, place = lax.optimization_barrier((offs, solved, weights, place))
    target = jnp.pad(offs, ((0, 0), (0, WIRE - half)), constant_values=-1.0).reshape(1, -1)
    selector = jnp.arange(pair_rows, dtype=jnp.int32)[:, None].astype(bf16) == target
    arrived = jnp.dot(
        selector.astype(bf16), got.reshape(-1, cols), preferred_element_type=f32
    ).reshape(2, piece, cols)
    rhs_cols = jnp.take(rhs_interface, column_order, axis=1)
    mine = jnp.arange(2)[:, None, None] == core
    own = jnp.where(mine, rhs_cols[None], 0.0) - arrived
    reduced = own + lax.ppermute(own, "c", [(0, 1), (1, 0)])
    reduced = reduced.reshape(pair_rows, cols).astype(bf16)
    z = lax.axis_index("z")
    depth = lax.axis_size("z")
    near = [reduced] + [shifted(reduced, "z", by) for by in range(1, depth)]
    section = jnp.concatenate(
        [lax.select_n((z - at) % depth, *near) for at in range(depth)], axis=0
    )

    product = jnp.dot(schur_inverse, section, preferred_element_type=f32)
    parts = exchange(product.astype(bf16).reshape(secs, piece, cols), SEC)
    summed = jnp.sum(parts.astype(f32), axis=0).astype(bf16)
    values = copies(summed, SEC).reshape(band, cols)

    s = lax.axis_index(SEC)
    asked = lax.dynamic_slice_in_dim(got[:, half + 1 : half + 3], s * devs, devs, axis=0)
    asked = lax.dynamic_slice_in_dim(jnp.concatenate([asked, asked]), me, devs, axis=0)
    asked = asked.reshape(devs, band // pair_rows, 64)[:, :, :per_pair]
    asked = jnp.swapaxes(asked, 0, 1).astype(f32).reshape(devs, 1, slots // devs)
    whole = pl.BlockSpec(memory_space=pltpu.VMEM)
    pieces = pl.pallas_call(
        serve_kernel,
        in_specs=[whole, whole],
        out_specs=[whole] * devs,
        out_shape=[jax.ShapeDtypeStruct((slots // devs, cols), bf16)] * devs,
        compiler_params=pltpu.CompilerParams(vmem_limit_bytes=16 << 20),
        cost_estimate=cost(2 * 10**8, 4 * 10**6),
        name="serve",
    )(asked, values)
    back = [pieces[0]] + [shifted(pieces[by], DEV, by) for by in range(1, devs)]
    interior = pl.pallas_call(
        tail_kernel,
        grid_spec=pltpu.PrefetchScalarGridSpec(
            num_scalar_prefetch=1,
            grid=(steps // CHUNKS,),
            in_specs=[
                *[pl.BlockSpec((slots // devs, cols), lambda i, at: (0, 0))] * devs,
                pl.BlockSpec((wide * n, cols), lambda i, at: (i, 0)),
                pl.BlockSpec((wide // 2, n, 2 * k), lambda i, at: (i, 0, 0)),
            ],
            out_specs=pl.BlockSpec((wide * n, cols), lambda i, at: (i, 0)),
            scratch_shapes=[
                pltpu.VMEM((2 * (slots + 8), 128), f32),
                pltpu.VMEM((2 * wide * k, 128), f32),
            ],
        ),
        out_shape=jax.ShapeDtypeStruct((nb * n, cols), bf16),
        cost_estimate=cost(4 * 10**9, 14 * 10**6),
        name="tail",
    )(place, *back, solved, weights)
    return interior, values.astype(f32)


def solution(mesh):
    fine = Mesh(mesh.devices.reshape(4, 4, 4, 2), ALL)
    placed = (
        P(ALL, None),
        P(ALL, None),
        P(ALL, None, None),
        P(ALL, None, None, None),
        P(ALL, None),
        P(ALL),
        P(),
        P(DEV, SEC),
    )
    return jax.shard_map(
        shards,
        mesh=fine,
        in_specs=placed,
        out_specs=(P(ALL, None), P(DEV, None)),
        check_vma=False,
    )
```

```python
import functools

import jax
import jax.numpy as jnp
from jax import lax
from jax.experimental import pallas as pl
from jax.experimental.pallas import tpu as pltpu
from jax.sharding import Mesh
from jax.sharding import PartitionSpec as P

ALL = ("y", "x", "z", "c")
SEC = ("y", "x")
DEV = ("z", "c")
WIRE = 24
GROUP = 4
CHUNKS = 2
BATCH = 10
F32, BF16 = jnp.float32, jnp.bfloat16


def exchange(blocks, axis):
    return lax.all_to_all(blocks, axis, 0, 0, tiled=True)


def copies(array, axis):
    size = lax.axis_size(axis)
    return exchange(jnp.broadcast_to(array[None], (size, *array.shape)), axis)


def shifted(array, axis, by):
    size = lax.axis_size(axis)
    return lax.ppermute(array, axis, [(i, (i + by) % size) for i in range(size)])


def iota(shape, dim):
    return lax.broadcasted_iota(jnp.int32, shape, dim).astype(F32)


def quotient(x, n):
    return jnp.floor((x + 0.5) * (1.0 / n))


def dot(a, b, dims=((1,), (0,))):
    return lax.dot_general(a, b, (dims, ((), ())), preferred_element_type=F32)


def onehot(mask):
    return jnp.where(mask, 1.0, 0.0).astype(BF16)


def forward_kernel(
    sizes, counts_ref, map_ref, rhs_ref, inv_ref, couple_ref, out_ref, place_ref,
    wide_ref, stage_ref, base_ref, offs_ref, wire_ref, at_ref, sem
):
    per_pair, half, pair_rows, pairs, devs = sizes
    step = pl.program_id(0)
    n = inv_ref.shape[1]
    k = couple_ref.shape[1]
    lanes = GROUP * k
    rows_out = out_ref.shape[0]

    def handover(slot):
        return pltpu.make_async_copy(wire_ref.at[slot], at_ref.at[slot], sem.at[slot])

    @pl.when(step == 0)
    def _():
        stage_ref[...] = jnp.zeros_like(stage_ref)
        base_ref[...] = jnp.zeros_like(base_ref)
        offs_ref[...] = jnp.zeros_like(offs_ref)
        wire_ref[1] = jnp.full((1, lanes), 2 * rows_out, jnp.int32)

    def move(slot, first, last):
        for i in range(first, last):
            row = pl.ds(pl.multiple_of(at_ref[slot, 0, i], 2), 2)
            wide_ref[row, :] = stage_ref[2 * i : 2 * i + 2, :]

    for now in range(CHUNKS):
        before, c0 = 1 - now, now * GROUP
        first = step * (CHUNKS * GROUP) + c0
        slot = jnp.concatenate(
            [map_ref[pl.ds(first + b, 1), :] for b in range(GROUP)], axis=1
        ).astype(F32)
        at = lax.broadcasted_iota(jnp.int32, (1, k), 1)
        live = jnp.concatenate(
            [jnp.where(at < counts_ref[first + b], 1.0, 0.0) for b in range(GROUP)], axis=1
        )
        pair = quotient(slot, pair_rows)
        off = slot - pair_rows * pair
        table = jnp.where(iota((pairs, lanes), 0) == pair, 1.0, 0.0)
        earlier = dot(
            table.astype(BF16), onehot(iota((lanes, lanes), 0) < iota((lanes, lanes), 1))
        )
        rank = jnp.sum(table * (earlier + base_ref[:, :1]), axis=0, keepdims=True)
        base_ref[...] += jnp.sum(table, axis=1, keepdims=True)
        place = pair * per_pair + rank
        place_ref[now] = (2.0 * jnp.where(live == 0.0, pairs * per_pair, place)).astype(jnp.int32)
        wire = place + (WIRE - half) * quotient(place, half)
        wire_ref[now] = (2.0 * wire).astype(jnp.int32)
        row64 = (lax.broadcasted_iota(jnp.int32, (256, lanes), 0) & 63).astype(F32)
        offs_ref[...] += dot((table * off).astype(BF16), onehot(row64 == rank), ((1,), (1,)))

        if now == 0:

            @pl.when(step == 0)
            def _():
                handover(1).start()

        solved = [
            dot(inv_ref[b], rhs_ref[b * n : (b + 1) * n, :]).astype(BF16)
            for b in range(c0, c0 + GROUP)
        ]
        handover(before).wait()
        handover(now).start()
        move(before, 0, lanes // 2)
        parts = [dot(couple_ref[c0 + b], solved[b]) for b in range(GROUP)]
        move(before, lanes // 2, lanes)
        depth = lax.broadcasted_iota(jnp.int32, (k, 2 * 128), 0)
        for b in range(GROUP):
            part = jnp.where(depth < counts_ref[first + b], parts[b], 0.0)
            stage_ref[pl.ds(2 * b * k, k, stride=2), :] = part[:, :128]
            stage_ref[pl.ds(2 * b * k + 1, k, stride=2), :] = part[:, 128:]

    @pl.when(step == pl.num_programs(0) - 1)
    def _():
        handover(1).wait()
        move(1, 0, lanes)
        offs = offs_ref[...]
        p = lax.broadcasted_iota(jnp.int32, offs.shape, 0)
        lane = lax.broadcasted_iota(jnp.int32, offs.shape, 1)
        spread = jnp.where((lane >> 6) == (p & 3), offs, 0.0).astype(BF16)
        groups = pairs // 4
        member = iota((groups, pairs), 0) == quotient(iota((groups, pairs), 1), 4)
        wanted = dot(onehot(member), spread)
        level = lax.broadcasted_iota(jnp.int32, (2 * (WIRE - half), 128), 0)

        def spread_rows(parts, rest):
            for at, part in parts:
                rest = jnp.where(level == at, jnp.broadcast_to(part, level.shape), rest)
            return rest

        for v in range(devs):
            rows = [wanted[2 * v + r : 2 * v + r + 1, :] for r in range(2)]
            fixed = spread_rows(
                [(2 + 2 * r + h, rows[r][:, 128 * h : 128 * (h + 1)]) for r in range(2) for h in range(2)],
                jnp.zeros(level.shape, F32),
            )
            for d in range(v, rows_out // WIRE, devs):
                own = [(h, offs_ref[d // 2 : d // 2 + 1, 128 * h : 128 * (h + 1)]) for h in range(2)]
                w = 2 * (d * WIRE + half)
                wide_ref[w : w + 2 * (WIRE - half), :] = spread_rows(own, fixed)
        for t in range(rows_out // 256):
            rows = slice(256 * t, 256 * (t + 1))
            for h in range(2):
                out_ref[rows, 128 * h : 128 * (h + 1)] = wide_ref[
                    pl.ds(512 * t + h, 256, stride=2), :
                ].astype(BF16)


def middle_kernel(rhs_ref, inv_ref, couple_ref, solved_ref, w_ref):
    n = inv_ref.shape[1]
    for b in range(GROUP):
        rows = slice(b * n, (b + 1) * n)
        solved_ref[rows, :] = dot(inv_ref[b], rhs_ref[rows, :]).astype(BF16)
    for b in range(0, GROUP, 2):
        w_ref[b // 2] = jnp.concatenate(
            [dot(inv_ref[c], couple_ref[c], ((1,), (1,))) for c in (b, b + 1)], axis=1
        ).astype(BF16)


def tail_kernel(place_ref, *refs):
    *back_refs, solved_ref, w_ref, out_ref, wide_ref, pick_ref = refs
    n = w_ref.shape[1]
    k = w_ref.shape[2] // 2
    group = 2 * w_ref.shape[0]
    share = back_refs[0].shape[0]
    slots = share * len(back_refs)
    lanes = group * k
    step = pl.program_id(0)

    def gather(step, first, last):
        here = place_ref.at[pl.ds(step * lanes, lanes)]
        for i in range(first, last):
            row = pl.ds(pl.multiple_of(here[i], 2), 2)
            pick_ref[2 * i : 2 * i + 2, :] = wide_ref[row, :]

    @pl.when(step == 0)
    def _():
        for t, back_ref in enumerate(back_refs):
            for h in range(2):
                wide_ref[pl.ds(2 * share * t + h, share, stride=2), :] = back_ref[
                    :, 128 * h : 128 * (h + 1)
                ].astype(F32)
        wide_ref[2 * slots :, :] = jnp.zeros_like(wide_ref[2 * slots :, :])
        gather(step, 0, lanes)

    picked = jnp.concatenate(
        [pick_ref[pl.ds(h, lanes, stride=2), :] for h in range(2)], axis=1
    ).astype(BF16)
    empty = jnp.zeros((k, picked.shape[1]), BF16)
    for b in range(group):
        rows = slice(b * n, (b + 1) * n)
        own = picked[b * k : (b + 1) * k, :]
        pad = [own, empty] if b % 2 == 0 else [empty, own]
        term = dot(w_ref[b // 2], jnp.concatenate(pad, axis=0))
        gather(step + 1, b * k, (b + 1) * k)
        out_ref[rows, :] = (solved_ref[rows, :].astype(F32) - term).astype(BF16)


def serve_kernel(asked_ref, values_ref, *returned_refs):
    peers = len(returned_refs)
    rows = returned_refs[0].shape[0]
    count = asked_ref.shape[2]
    per_pair = rows // peers
    depth = values_ref.shape[0] // peers
    for j in range(peers):
        picker = onehot(asked_ref[j] == iota((depth, count), 0))
        chosen = dot(picker, values_ref[j * depth : (j + 1) * depth, :], ((0,), (0,)))
        for v in range(peers):
            part = chosen[v * per_pair : (v + 1) * per_pair, :]
            returned_refs[v][j * per_pair : (j + 1) * per_pair, :] = part.astype(BF16)


def cost(flops, size):
    return pl.CostEstimate(flops=flops, bytes_accessed=size, transcendentals=0)


def shards(
    rhs_interior,
    rhs_interface,
    inv_blocks,
    coupling,
    interface_map,
    slot_counts,
    column_order,
    schur_inverse,
):
    f32, bf16 = F32, BF16
    nb, n = inv_blocks.shape[:2]
    k = coupling.shape[2]
    cols = rhs_interior.shape[1]
    owners = lax.axis_size(ALL)
    devs = lax.axis_size(DEV)
    secs = lax.axis_size(SEC)
    pairs = owners // 2
    slots = nb * k
    per_pair = slots // pairs
    half = per_pair // 2
    piece = rhs_interface.shape[0]
    pair_rows = 2 * piece
    band = piece * secs
    steps = nb // GROUP
    lanes = GROUP * k

    block_specs = [
        pl.BlockSpec((GROUP * n, cols), lambda i: (i, 0)),
        pl.BlockSpec((GROUP, n, n), lambda i: (i, 0, 0)),
    ]
    wide = CHUNKS * GROUP
    sent, place = pl.pallas_call(
        functools.partial(forward_kernel, (per_pair, half, pair_rows, pairs, devs)),
        grid_spec=pltpu.PrefetchScalarGridSpec(
            num_scalar_prefetch=1,
            grid=(steps // CHUNKS,),
            in_specs=[
                pl.BlockSpec((nb, k), lambda i, at: (0, 0)),
                pl.BlockSpec((wide * n, cols), lambda i, at: (i, 0)),
                pl.BlockSpec((wide, n, n), lambda i, at: (i, 0, 0)),
                pl.BlockSpec((wide, None, k, n), lambda i, at: (i, 0, 0, 0)),
            ],
            out_specs=[
                pl.BlockSpec((owners * WIRE, cols), lambda i, at: (0, 0)),
                pl.BlockSpec((CHUNKS, 1, lanes), lambda i, at: (i, 0, 0)),
            ],
            scratch_shapes=[
                pltpu.VMEM((2 * (owners * WIRE + 8), 128), f32),
                pltpu.VMEM((2 * lanes, 128), f32),
                pltpu.VMEM((pairs, 128), f32),
                pltpu.VMEM((pairs, 256), f32),
                pltpu.VMEM((2, 1, lanes), jnp.int32),
                pltpu.SMEM((2, 1, lanes), jnp.int32),
                pltpu.SemaphoreType.DMA((2,)),
            ],
        ),
        out_shape=[
            jax.ShapeDtypeStruct((owners * WIRE, cols), bf16),
            jax.ShapeDtypeStruct((steps, 1, lanes), jnp.int32),
        ],
        cost_estimate=cost(2 * 10**9, 14 * 10**6),
        name="forward",
    )(slot_counts, interface_map, rhs_interior, inv_blocks, coupling)
    got = exchange(sent.reshape(owners, WIRE, cols), ALL)
    solved, weights = pl.pallas_call(
        middle_kernel,
        grid=(steps,),
        in_specs=[*block_specs, pl.BlockSpec((GROUP, None, k, n), lambda i: (i, 1, 0, 0))],
        out_specs=[
            pl.BlockSpec((GROUP * n, cols), lambda i: (i, 0)),
            pl.BlockSpec((GROUP // 2, n, 2 * k), lambda i: (i, 0, 0)),
        ],
        out_shape=[
            jax.ShapeDtypeStruct((nb * n, cols), bf16),
            jax.ShapeDtypeStruct((nb // 2, n, 2 * k), bf16),
        ],
        cost_estimate=cost(2 * 10**9, 20 * 10**6),
        name="middle",
    )(rhs_interior, inv_blocks, coupling)

    core = lax.axis_index("c")
    offs = jnp.where(core == 0, got[:, half, :half], got[:, half, half : 2 * half])
    me = lax.axis_index(DEV)
    share = 2 * slots // devs
    nearer = (me - place // share) % devs * share + place % share
    place = jnp.where(place < 2 * slots, nearer, place).reshape(-1)
    place = jnp.pad(place, (0, BATCH * k), constant_values=2 * slots)
    offs, solved, weights, place = lax.optimization_barrier((offs, solved, weights, place))
    target = jnp.pad(offs, ((0, 0), (0, WIRE - half)), constant_values=-1.0).reshape(1, -1)
    selector = jnp.arange(pair_rows, dtype=jnp.int32)[:, None].astype(bf16) == target
    arrived = jnp.dot(
        selector.astype(bf16), got.reshape(-1, cols), preferred_element_type=f32
    ).reshape(2, piece, cols)
    rhs_cols = jnp.take(rhs_interface, column_order, axis=1)
    mine = jnp.arange(2)[:, None, None] == core
    own = jnp.where(mine, rhs_cols[None], 0.0) - arrived
    reduced = own + lax.ppermute(own, "c", [(0, 1), (1, 0)])
    reduced = reduced.reshape(pair_rows, cols).astype(bf16)
    z = lax.axis_index("z")
    depth = lax.axis_size("z")
    near = [reduced] + [shifted(reduced, "z", by) for by in range(1, depth)]
    section = jnp.concatenate(
        [lax.select_n((z - at) % depth, *near) for at in range(depth)], axis=0
    )

    product = jnp.dot(schur_inverse, section, preferred_element_type=f32)
    parts = exchange(product.astype(bf16).reshape(secs, piece, cols), SEC)
    summed = jnp.sum(parts.astype(f32), axis=0).astype(bf16)
    values = copies(summed, SEC).reshape(band, cols)

    s = lax.axis_index(SEC)
    asked = lax.dynamic_slice_in_dim(got[:, half + 1 : half + 3], s * devs, devs, axis=0)
    asked = lax.dynamic_slice_in_dim(jnp.concatenate([asked, asked]), me, devs, axis=0)
    asked = asked.reshape(devs, band // pair_rows, 64)[:, :, :per_pair]
    asked = jnp.swapaxes(asked, 0, 1).astype(f32).reshape(devs, 1, slots // devs)
    whole = pl.BlockSpec(memory_space=pltpu.VMEM)
    pieces = pl.pallas_call(
        serve_kernel,
        in_specs=[whole, whole],
        out_specs=[whole] * devs,
        out_shape=[jax.ShapeDtypeStruct((slots // devs, cols), bf16)] * devs,
        compiler_params=pltpu.CompilerParams(vmem_limit_bytes=16 << 20),
        cost_estimate=cost(2 * 10**8, 4 * 10**6),
        name="serve",
    )(asked, values)
    back = [pieces[0]] + [shifted(pieces[by], DEV, by) for by in range(1, devs)]
    batch = BATCH
    interior = pl.pallas_call(
        tail_kernel,
        grid_spec=pltpu.PrefetchScalarGridSpec(
            num_scalar_prefetch=1,
            grid=(nb // batch,),
            in_specs=[
                *[pl.BlockSpec((slots // devs, cols), lambda i, at: (0, 0))] * devs,
                pl.BlockSpec((batch * n, cols), lambda i, at: (i, 0)),
                pl.BlockSpec((batch // 2, n, 2 * k), lambda i, at: (i, 0, 0)),
            ],
            out_specs=pl.BlockSpec((batch * n, cols), lambda i, at: (i, 0)),
            scratch_shapes=[
                pltpu.VMEM((2 * (slots + 8), 128), f32),
                pltpu.VMEM((2 * batch * k, 128), f32),
            ],
        ),
        out_shape=jax.ShapeDtypeStruct((nb * n, cols), bf16),
        cost_estimate=cost(4 * 10**9, 14 * 10**6),
        name="tail",
    )(place, *back, solved, weights)
    return interior, values.astype(f32)


def solution(mesh):
    fine = Mesh(mesh.devices.reshape(4, 4, 4, 2), ALL)
    placed = (
        P(ALL, None),
        P(ALL, None),
        P(ALL, None, None),
        P(ALL, None, None, None),
        P(ALL, None),
        P(ALL),
        P(),
        P(DEV, SEC),
    )
    return jax.shard_map(
        shards,
        mesh=fine,
        in_specs=placed,
        out_specs=(P(ALL, None), P(DEV, None)),
        check_vma=False,
    )
```

```python
import functools

import jax
import jax.numpy as jnp
from jax import lax
from jax.experimental import pallas as pl
from jax.experimental.pallas import tpu as pltpu
from jax.sharding import Mesh
from jax.sharding import PartitionSpec as P

ALL = ("y", "x", "z", "c")
SEC = ("y", "x")
DEV = ("z", "c")
WIRE = 24
GROUP = 4
CHUNKS = 2
BATCH = 20
F32, BF16 = jnp.float32, jnp.bfloat16


def exchange(blocks, axis):
    return lax.all_to_all(blocks, axis, 0, 0, tiled=True)


def copies(array, axis):
    size = lax.axis_size(axis)
    return exchange(jnp.broadcast_to(array[None], (size, *array.shape)), axis)


def shifted(array, axis, by):
    size = lax.axis_size(axis)
    return lax.ppermute(array, axis, [(i, (i + by) % size) for i in range(size)])


def iota(shape, dim):
    return lax.broadcasted_iota(jnp.int32, shape, dim).astype(F32)


def quotient(x, n):
    return jnp.floor((x + 0.5) * (1.0 / n))


def dot(a, b, dims=((1,), (0,))):
    return lax.dot_general(a, b, (dims, ((), ())), preferred_element_type=F32)


def onehot(mask):
    return jnp.where(mask, 1.0, 0.0).astype(BF16)


def forward_kernel(
    sizes, counts_ref, map_ref, rhs_ref, inv_ref, couple_ref, out_ref, place_ref,
    wide_ref, stage_ref, base_ref, offs_ref, wire_ref, at_ref, sem
):
    per_pair, half, pair_rows, pairs, devs = sizes
    step = pl.program_id(0)
    n = inv_ref.shape[1]
    k = couple_ref.shape[1]
    lanes = GROUP * k
    rows_out = out_ref.shape[0]

    def handover(slot):
        return pltpu.make_async_copy(wire_ref.at[slot], at_ref.at[slot], sem.at[slot])

    @pl.when(step == 0)
    def _():
        stage_ref[...] = jnp.zeros_like(stage_ref)
        base_ref[...] = jnp.zeros_like(base_ref)
        offs_ref[...] = jnp.zeros_like(offs_ref)
        wire_ref[1] = jnp.full((1, lanes), 2 * rows_out, jnp.int32)

    def move(slot, first, last):
        for i in range(first, last):
            row = pl.ds(pl.multiple_of(at_ref[slot, 0, i], 2), 2)
            wide_ref[row, :] = stage_ref[2 * i : 2 * i + 2, :]

    for now in range(CHUNKS):
        before, c0 = 1 - now, now * GROUP
        first = step * (CHUNKS * GROUP) + c0
        slot = jnp.concatenate(
            [map_ref[pl.ds(first + b, 1), :] for b in range(GROUP)], axis=1
        ).astype(F32)
        at = lax.broadcasted_iota(jnp.int32, (1, k), 1)
        live = jnp.concatenate(
            [jnp.where(at < counts_ref[first + b], 1.0, 0.0) for b in range(GROUP)], axis=1
        )
        pair = quotient(slot, pair_rows)
        off = slot - pair_rows * pair
        table = jnp.where(iota((pairs, lanes), 0) == pair, 1.0, 0.0)
        earlier = dot(
            table.astype(BF16), onehot(iota((lanes, lanes), 0) < iota((lanes, lanes), 1))
        )
        rank = jnp.sum(table * (earlier + base_ref[:, :1]), axis=0, keepdims=True)
        base_ref[...] += jnp.sum(table, axis=1, keepdims=True)
        place = pair * per_pair + rank
        place_ref[now] = (2.0 * jnp.where(live == 0.0, pairs * per_pair, place)).astype(jnp.int32)
        wire = place + (WIRE - half) * quotient(place, half)
        wire_ref[now] = (2.0 * wire).astype(jnp.int32)
        row64 = (lax.broadcasted_iota(jnp.int32, (256, lanes), 0) & 63).astype(F32)
        offs_ref[...] += dot((table * off).astype(BF16), onehot(row64 == rank), ((1,), (1,)))

        if now == 0:

            @pl.when(step == 0)
            def _():
                handover(1).start()

        solved = [
            dot(inv_ref[b], rhs_ref[b * n : (b + 1) * n, :]).astype(BF16)
            for b in range(c0, c0 + GROUP)
        ]
        handover(before).wait()
        handover(now).start()
        move(before, 0, lanes // 2)
        parts = [dot(couple_ref[c0 + b], solved[b]) for b in range(GROUP)]
        move(before, lanes // 2, lanes)
        depth = lax.broadcasted_iota(jnp.int32, (k, 2 * 128), 0)
        for b in range(GROUP):
            part = jnp.where(depth < counts_ref[first + b], parts[b], 0.0)
            stage_ref[pl.ds(2 * b * k, k, stride=2), :] = part[:, :128]
            stage_ref[pl.ds(2 * b * k + 1, k, stride=2), :] = part[:, 128:]

    @pl.when(step == pl.num_programs(0) - 1)
    def _():
        handover(1).wait()
        move(1, 0, lanes)
        offs = offs_ref[...]
        p = lax.broadcasted_iota(jnp.int32, offs.shape, 0)
        lane = lax.broadcasted_iota(jnp.int32, offs.shape, 1)
        spread = jnp.where((lane >> 6) == (p & 3), offs, 0.0).astype(BF16)
        groups = pairs // 4
        member = iota((groups, pairs), 0) == quotient(iota((groups, pairs), 1), 4)
        wanted = dot(onehot(member), spread)
        level = lax.broadcasted_iota(jnp.int32, (2 * (WIRE - half), 128), 0)

        def spread_rows(parts, rest):
            for at, part in parts:
                rest = jnp.where(level == at, jnp.broadcast_to(part, level.shape), rest)
            return rest

        for v in range(devs):
            rows = [wanted[2 * v + r : 2 * v + r + 1, :] for r in range(2)]
            fixed = spread_rows(
                [(2 + 2 * r + h, rows[r][:, 128 * h : 128 * (h + 1)]) for r in range(2) for h in range(2)],
                jnp.zeros(level.shape, F32),
            )
            for d in range(v, rows_out // WIRE, devs):
                own = [(h, offs_ref[d // 2 : d // 2 + 1, 128 * h : 128 * (h + 1)]) for h in range(2)]
                w = 2 * (d * WIRE + half)
                wide_ref[w : w + 2 * (WIRE - half), :] = spread_rows(own, fixed)
        for t in range(rows_out // 256):
            rows = slice(256 * t, 256 * (t + 1))
            for h in range(2):
                out_ref[rows, 128 * h : 128 * (h + 1)] = wide_ref[
                    pl.ds(512 * t + h, 256, stride=2), :
                ].astype(BF16)


def middle_kernel(rhs_ref, inv_ref, couple_ref, solved_ref, w_ref):
    n = inv_ref.shape[1]
    for b in range(GROUP):
        rows = slice(b * n, (b + 1) * n)
        solved_ref[rows, :] = dot(inv_ref[b], rhs_ref[rows, :]).astype(BF16)
    for b in range(0, GROUP, 2):
        w_ref[b // 2] = jnp.concatenate(
            [dot(inv_ref[c], couple_ref[c], ((1,), (1,))) for c in (b, b + 1)], axis=1
        ).astype(BF16)


def tail_kernel(place_ref, *refs):
    *back_refs, solved_ref, w_ref, out_ref, wide_ref, pick_ref = refs
    n = w_ref.shape[1]
    k = w_ref.shape[2] // 2
    group = 2 * w_ref.shape[0]
    share = back_refs[0].shape[0]
    slots = share * len(back_refs)
    lanes = group * k
    step = pl.program_id(0)

    def gather(step, first, last):
        here = place_ref.at[pl.ds(step * lanes, lanes)]
        for i in range(first, last):
            row = pl.ds(pl.multiple_of(here[i], 2), 2)
            pick_ref[2 * i : 2 * i + 2, :] = wide_ref[row, :]

    @pl.when(step == 0)
    def _():
        for t, back_ref in enumerate(back_refs):
            for h in range(2):
                wide_ref[pl.ds(2 * share * t + h, share, stride=2), :] = back_ref[
                    :, 128 * h : 128 * (h + 1)
                ].astype(F32)
        wide_ref[2 * slots :, :] = jnp.zeros_like(wide_ref[2 * slots :, :])
        gather(step, 0, lanes)

    picked = jnp.concatenate(
        [pick_ref[pl.ds(h, lanes, stride=2), :] for h in range(2)], axis=1
    ).astype(BF16)
    empty = jnp.zeros((k, picked.shape[1]), BF16)
    for b in range(group):
        rows = slice(b * n, (b + 1) * n)
        own = picked[b * k : (b + 1) * k, :]
        pad = [own, empty] if b % 2 == 0 else [empty, own]
        term = dot(w_ref[b // 2], jnp.concatenate(pad, axis=0))
        gather(step + 1, b * k, (b + 1) * k)
        out_ref[rows, :] = (solved_ref[rows, :].astype(F32) - term).astype(BF16)


def serve_kernel(asked_ref, values_ref, *returned_refs):
    peers = len(returned_refs)
    rows = returned_refs[0].shape[0]
    count = asked_ref.shape[2]
    per_pair = rows // peers
    depth = values_ref.shape[0] // peers
    for j in range(peers):
        picker = onehot(asked_ref[j] == iota((depth, count), 0))
        chosen = dot(picker, values_ref[j * depth : (j + 1) * depth, :], ((0,), (0,)))
        for v in range(peers):
            part = chosen[v * per_pair : (v + 1) * per_pair, :]
            returned_refs[v][j * per_pair : (j + 1) * per_pair, :] = part.astype(BF16)


def cost(flops, size):
    return pl.CostEstimate(flops=flops, bytes_accessed=size, transcendentals=0)


def shards(
    rhs_interior,
    rhs_interface,
    inv_blocks,
    coupling,
    interface_map,
    slot_counts,
    column_order,
    schur_inverse,
):
    f32, bf16 = F32, BF16
    nb, n = inv_blocks.shape[:2]
    k = coupling.shape[2]
    cols = rhs_interior.shape[1]
    owners = lax.axis_size(ALL)
    devs = lax.axis_size(DEV)
    secs = lax.axis_size(SEC)
    pairs = owners // 2
    slots = nb * k
    per_pair = slots // pairs
    half = per_pair // 2
    piece = rhs_interface.shape[0]
    pair_rows = 2 * piece
    band = piece * secs
    steps = nb // GROUP
    lanes = GROUP * k

    block_specs = [
        pl.BlockSpec((GROUP * n, cols), lambda i: (i, 0)),
        pl.BlockSpec((GROUP, n, n), lambda i: (i, 0, 0)),
    ]
    wide = CHUNKS * GROUP
    sent, place = pl.pallas_call(
        functools.partial(forward_kernel, (per_pair, half, pair_rows, pairs, devs)),
        grid_spec=pltpu.PrefetchScalarGridSpec(
            num_scalar_prefetch=1,
            grid=(steps // CHUNKS,),
            in_specs=[
                pl.BlockSpec((nb, k), lambda i, at: (0, 0)),
                pl.BlockSpec((wide * n, cols), lambda i, at: (i, 0)),
                pl.BlockSpec((wide, n, n), lambda i, at: (i, 0, 0)),
                pl.BlockSpec((wide, None, k, n), lambda i, at: (i, 0, 0, 0)),
            ],
            out_specs=[
                pl.BlockSpec((owners * WIRE, cols), lambda i, at: (0, 0)),
                pl.BlockSpec((CHUNKS, 1, lanes), lambda i, at: (i, 0, 0)),
            ],
            scratch_shapes=[
                pltpu.VMEM((2 * (owners * WIRE + 8), 128), f32),
                pltpu.VMEM((2 * lanes, 128), f32),
                pltpu.VMEM((pairs, 128), f32),
                pltpu.VMEM((pairs, 256), f32),
                pltpu.VMEM((2, 1, lanes), jnp.int32),
                pltpu.SMEM((2, 1, lanes), jnp.int32),
                pltpu.SemaphoreType.DMA((2,)),
            ],
        ),
        out_shape=[
            jax.ShapeDtypeStruct((owners * WIRE, cols), bf16),
            jax.ShapeDtypeStruct((steps, 1, lanes), jnp.int32),
        ],
        cost_estimate=cost(2 * 10**9, 14 * 10**6),
        name="forward",
    )(slot_counts, interface_map, rhs_interior, inv_blocks, coupling)
    got = exchange(sent.reshape(owners, WIRE, cols), ALL)
    solved, weights = pl.pallas_call(
        middle_kernel,
        grid=(steps,),
        in_specs=[*block_specs, pl.BlockSpec((GROUP, None, k, n), lambda i: (i, 1, 0, 0))],
        out_specs=[
            pl.BlockSpec((GROUP * n, cols), lambda i: (i, 0)),
            pl.BlockSpec((GROUP // 2, n, 2 * k), lambda i: (i, 0, 0)),
        ],
        out_shape=[
            jax.ShapeDtypeStruct((nb * n, cols), bf16),
            jax.ShapeDtypeStruct((nb // 2, n, 2 * k), bf16),
        ],
        cost_estimate=cost(2 * 10**9, 20 * 10**6),
        name="middle",
    )(rhs_interior, inv_blocks, coupling)

    core = lax.axis_index("c")
    offs = jnp.where(core == 0, got[:, half, :half], got[:, half, half : 2 * half])
    me = lax.axis_index(DEV)
    share = 2 * slots // devs
    nearer = (me - place // share) % devs * share + place % share
    place = jnp.where(place < 2 * slots, nearer, place).reshape(-1)
    place = jnp.pad(place, (0, BATCH * k), constant_values=2 * slots)
    offs, solved, weights, place = lax.optimization_barrier((offs, solved, weights, place))
    target = jnp.pad(offs, ((0, 0), (0, WIRE - half)), constant_values=-1.0).reshape(1, -1)
    selector = jnp.arange(pair_rows, dtype=jnp.int32)[:, None].astype(bf16) == target
    arrived = jnp.dot(
        selector.astype(bf16), got.reshape(-1, cols), preferred_element_type=f32
    ).reshape(2, piece, cols)
    rhs_cols = jnp.take(rhs_interface, column_order, axis=1)
    mine = jnp.arange(2)[:, None, None] == core
    own = jnp.where(mine, rhs_cols[None], 0.0) - arrived
    reduced = own + lax.ppermute(own, "c", [(0, 1), (1, 0)])
    reduced = reduced.reshape(pair_rows, cols).astype(bf16)
    z = lax.axis_index("z")
    depth = lax.axis_size("z")
    near = [reduced] + [shifted(reduced, "z", by) for by in range(1, depth)]
    section = jnp.concatenate(
        [lax.select_n((z - at) % depth, *near) for at in range(depth)], axis=0
    )

    product = jnp.dot(schur_inverse, section, preferred_element_type=f32)
    parts = exchange(product.astype(bf16).reshape(secs, piece, cols), SEC)
    summed = jnp.sum(parts.astype(f32), axis=0).astype(bf16)
    values = copies(summed, SEC).reshape(band, cols)

    s = lax.axis_index(SEC)
    asked = lax.dynamic_slice_in_dim(got[:, half + 1 : half + 3], s * devs, devs, axis=0)
    asked = lax.dynamic_slice_in_dim(jnp.concatenate([asked, asked]), me, devs, axis=0)
    asked = asked.reshape(devs, band // pair_rows, 64)[:, :, :per_pair]
    asked = jnp.swapaxes(asked, 0, 1).astype(f32).reshape(devs, 1, slots // devs)
    whole = pl.BlockSpec(memory_space=pltpu.VMEM)
    pieces = pl.pallas_call(
        serve_kernel,
        in_specs=[whole, whole],
        out_specs=[whole] * devs,
        out_shape=[jax.ShapeDtypeStruct((slots // devs, cols), bf16)] * devs,
        compiler_params=pltpu.CompilerParams(vmem_limit_bytes=16 << 20),
        cost_estimate=cost(2 * 10**8, 4 * 10**6),
        name="serve",
    )(asked, values)
    back = [pieces[0]] + [shifted(pieces[by], DEV, by) for by in range(1, devs)]
    batch = BATCH
    interior = pl.pallas_call(
        tail_kernel,
        grid_spec=pltpu.PrefetchScalarGridSpec(
            num_scalar_prefetch=1,
            grid=(nb // batch,),
            in_specs=[
                *[pl.BlockSpec((slots // devs, cols), lambda i, at: (0, 0))] * devs,
                pl.BlockSpec((batch * n, cols), lambda i, at: (i, 0)),
                pl.BlockSpec((batch // 2, n, 2 * k), lambda i, at: (i, 0, 0)),
            ],
            out_specs=pl.BlockSpec((batch * n, cols), lambda i, at: (i, 0)),
            scratch_shapes=[
                pltpu.VMEM((2 * (slots + 8), 128), f32),
                pltpu.VMEM((2 * batch * k, 128), f32),
            ],
        ),
        out_shape=jax.ShapeDtypeStruct((nb * n, cols), bf16),
        cost_estimate=cost(4 * 10**9, 14 * 10**6),
        name="tail",
    )(place, *back, solved, weights)
    return interior, values.astype(f32)


def solution(mesh):
    fine = Mesh(mesh.devices.reshape(4, 4, 4, 2), ALL)
    placed = (
        P(ALL, None),
        P(ALL, None),
        P(ALL, None, None),
        P(ALL, None, None, None),
        P(ALL, None),
        P(ALL),
        P(),
        P(DEV, SEC),
    )
    return jax.shard_map(
        shards,
        mesh=fine,
        in_specs=placed,
        out_specs=(P(ALL, None), P(DEV, None)),
        check_vma=False,
    )
```
